128 devices in a mesh: gx: 32 (over y, x_hi, z), gy: 4 (over x_lo, core).
Axes of the slice: x: 4 (x_hi: 2, x_lo: 2; x = x_hi * 2 + x_lo), y: 4, z: 4, core: 2. Of those that a mesh axis runs over, the one named last changes fastest.
Arguments:
- density: float32 [512, 128, 512], P('gx', 'gy'), may hold values from -6 to 6
- kernel: bfloat16 [16, 512], replicated, may hold values from -0.125 to 0.125
- electrode: int32 [512], P('gx'), may hold values from 0 to 15
- drift_sign: int32 [8], replicated, may hold values from 0 to 1
Outputs:
- final_density: float32 [512, 128, 512], P('gx', 'gy')
The draws below stay inside these ranges and needn't reach their ends.
Inputs may be any that keep to these rules, and one draw needn't show every extreme that they name: `electrode`: index into the voltage table. `drift_sign`: 1 makes positive momentum offsets drift toward higher y, 0 toward lower y.
All inputs are finite; a program needn't handle non-finite values.
Results may differ from the reference program's by a relative error of at most 0.024.
Values may be sent and summed in bfloat16 or wider, within the bound.
A program may use at most 192 MiB of HBM per device.

```python
import math
import jax
import jax.numpy as jnp
from jax import lax

NX = 512
NP = 512
YSLAB = 16
NV = 16
YSUB = 4
STEPS = 2
NY = 128
REACH = 128


def place_ends(values, stream_key, low, largest):
    place = [jax.random.randint(jax.random.fold_in(stream_key, axis), (), 0, length) for axis, length in enumerate(values.shape)]
    main_axis = values.shape.index(max(values.shape))
    neighbour = place[:main_axis] + [(place[main_axis] + 1) % values.shape[main_axis]] + place[main_axis + 1:]
    return values.at[tuple(place)].set(low).at[tuple(neighbour)].set(largest)


def block_scale(own_key, dims, shards, smallest, largest):
    def one(dim, shards_of):
        heights = jax.random.uniform(jax.random.fold_in(jax.random.fold_in(own_key, 6), dim), (shards_of,), jnp.float32, smallest / len(shards), largest / len(shards))
        return jnp.repeat(jnp.exp(heights), dims[dim] // shards_of).reshape((-1,) + (1,) * (len(dims) - dim - 1))

    factor_of = one(*shards[0])
    for cut in shards[1:]:
        factor_of = factor_of * one(*cut)
    return factor_of


def bell_draw(rng, extent, width, limit, cuts=(), kind=jnp.bfloat16):
    entries = width * jax.random.normal(rng, extent, jnp.float32)
    if cuts:
        entries = entries * block_scale(rng, extent, cuts, -0.22, 0.18)
    return jnp.clip(entries, -limit, limit).astype(kind)


def setup_inputs(seed: int = 0) -> dict:
    key_of = jax.random.split(jax.random.key(seed), 5)
    density = bell_draw(key_of[0], (NX, NY, NP), 1.0, 6.0, ((0, 32), (1, 4)), jnp.float32)
    kernel = bell_draw(key_of[1], (NV, NP), (4 * NP) ** -0.5, 0.125)
    electrode = place_ends(jax.random.randint(key_of[2], (NX,), 0, NV), jax.random.fold_in(key_of[2], 1), 0, NV - 1).astype(jnp.int32)
    drift_sign = place_ends(jax.random.randint(key_of[3], (NY // YSLAB,), 0, 2), jax.random.fold_in(key_of[3], 1), 0, 1).astype(jnp.int32)
    return {"density": density, "kernel": kernel, "electrode": electrode, "drift_sign": drift_sign}


drift_courant = 0.5


def fourier_table(total):
    index = jnp.arange(total, dtype=jnp.int32)
    product = (index[:, None] * index[None, :]) % total
    angle = (2.0 * math.pi / total) * product.astype(jnp.float32)
    return jnp.concatenate([jnp.cos(angle), jnp.sin(angle)], axis=0).astype(jnp.bfloat16)


def phase_factors(momentum_index, reach_cells, momentum_total, total):
    freq = jnp.arange(total, dtype=jnp.int32)
    kappa = jnp.where(freq > total // 2, freq - total, freq)
    offsets = (reach_cells * (momentum_total - 1 - 2 * momentum_index)).astype(jnp.int32)
    product = kappa[:, None] * offsets[None, :]
    modulus = total * momentum_total
    wrapped = product % modulus
    angle = (2.0 * math.pi / modulus) * wrapped.astype(jnp.float32)
    return jnp.cos(angle), jnp.sin(angle)


def x_advect(current):
    table = fourier_table(NX)
    cos_phase, sin_phase = phase_factors(jnp.arange(NP, dtype=jnp.int32), REACH, NP, NX)
    rounded = current.astype(jnp.bfloat16)

    def per_momentum(operands):
        column, cos_col, sin_col = operands
        spectra = jnp.dot(table, column, preferred_element_type=jnp.float32)
        real_part = spectra[:NX]
        imag_part = spectra[NX:]
        cos_col = cos_col[:, None]
        sin_col = sin_col[:, None]
        rotated = jnp.concatenate([real_part * cos_col - imag_part * sin_col, real_part * sin_col + imag_part * cos_col], axis=0).astype(jnp.bfloat16)
        return jnp.dot(table.T, rotated, preferred_element_type=jnp.float32) * (1.0 / NX)

    result = lax.map(per_momentum, (jnp.moveaxis(rounded, 1, 0), cos_phase.T, sin_phase.T))
    return jnp.moveaxis(result, 0, 1)


def y_drift(current, drift_sign):
    cell_index = jnp.arange(NY, dtype=jnp.int32)
    cell_sign = (2 * drift_sign[cell_index // YSLAB] - 1).astype(jnp.float32)
    face_index = jnp.arange(NY + 1, dtype=jnp.int32)
    face_sign = cell_sign[jnp.maximum(face_index - 1, 0)]
    momentum_factor = (2 * jnp.arange(NP, dtype=jnp.int32) - NP + 1).astype(jnp.float32) / NP
    face_speed = drift_courant * momentum_factor[:, None] * face_sign[None, :]

    def per_row(row_values):
        for sweep_index in range(YSUB):
            padded = jnp.pad(row_values, ((0, 0), (1, 1)))
            face_flux = jnp.maximum(face_speed, 0.0) * padded[:, :-1] + jnp.minimum(face_speed, 0.0) * padded[:, 1:]
            row_values = row_values - (face_flux[:, 1:] - face_flux[:, :-1])
        return row_values

    return lax.map(per_row, current)


def kick(current, electrode, kernel):
    momentum = jnp.arange(NP, dtype=jnp.int32)
    offset_grid = momentum[:, None] - momentum[None, :]
    distance = jnp.abs(offset_grid)

    def per_row(operands):
        column, setting = operands
        row_kernel = kernel[setting]
        gathered = row_kernel[distance]
        toeplitz = jnp.where(offset_grid >= 0, gathered, -gathered)
        slope_first = jnp.dot(toeplitz, column.astype(jnp.bfloat16), preferred_element_type=jnp.float32)
        midpoint = (column + 0.5 * slope_first).astype(jnp.bfloat16)
        slope_second = jnp.dot(toeplitz, midpoint, preferred_element_type=jnp.float32)
        return column + slope_second

    return lax.map(per_row, (current, electrode))


def reference(density, kernel, electrode, drift_sign):
    current = jnp.swapaxes(density, 1, 2)
    for section_index in range(STEPS):
        current = x_advect(current)
        current = y_drift(current, drift_sign)
        current = kick(current, electrode, kernel)
        current = x_advect(current)
    return jnp.swapaxes(current, 1, 2)
```

```python
import functools

import jax
import jax.numpy as jnp
import numpy as np
from jax import lax
from jax.experimental import pallas as pl
from jax.experimental.pallas import tpu as pltpu
from jax.sharding import PartitionSpec as P

NX = 512
NP = 512
XB = 16
YB = 32
NV = 16
PARTS = 128
MESH = pl.DeviceIdType.MESH
F32 = jnp.float32
BF16 = jnp.bfloat16


def shift_kernels():
    k = np.arange(NX)
    kappa = np.where(k > NX // 2, k - NX, k).astype(np.int64)
    n = np.arange(NX)
    rows = np.zeros((8, NX), np.float64)
    for parity in range(2):
        p = parity
        m = (kappa * (NX // 4) * (NP - 1 - 2 * p)) % (NX * NP)
        phase = 2 * np.pi * m / (NX * NP)
        g = np.cos(2 * np.pi * ((n[:, None] * k[None, :]) % NX) / NX - phase[None, :]).sum(1) / NX
        spectrum = np.fft.fft(g)
        g2 = np.fft.ifft(spectrum * spectrum).real
        whole = 127 - p // 2
        whole2 = 255 - p
        rows[parity] = np.roll(g, -whole)[(-n) % NX]
        rows[2 + parity] = np.roll(g2, -whole2)[(-n) % NX]
    return rows.astype(np.float32)


def send_order():
    ring = lambda t: min(t, 4 - t)
    offsets = [o for o in range(64)]
    key = lambda o: -(ring(o // 16) + ring(o // 4 % 4) + ring(o % 4))
    offsets.sort(key=lambda o: (key(o), (o * 37) % 64))
    offsets = offsets[:63]
    packed = []
    for i in range(0, 63, 3):
        trio = offsets[i : i + 3]
        packed.append(trio[0] + 64 * trio[1] + 4096 * trio[2])
    return packed


ORDER = send_order()


def for_each_peer(me, visit):
    y, z, x, core = me

    def group(g, carry):
        code = jnp.int32(0)
        for i, value in enumerate(ORDER):
            code = jnp.where(g == i, jnp.int32(value), code)

        def one(_, code):
            o = lax.rem(code, 64)
            y2 = lax.rem(y + o // 16, 4)
            z2 = lax.rem(z + lax.rem(o // 4, 4), 4)
            x2 = lax.rem(x + lax.rem(o, 4), 4)
            gx = y2 * 8 + (x2 // 2) * 4 + z2
            gy = lax.rem(x2, 2) * 2
            visit(gx, gy)
            visit(gx, gy + 1)
            return code // 64

        lax.fori_loop(0, 3, one, code)
        return carry

    lax.fori_loop(0, len(ORDER), group, 0)
    gx = y * 8 + (x // 2) * 4 + z
    visit(gx, lax.rem(x, 2) * 2 + 1 - core)


def iota(shape, axis):
    return lax.broadcasted_iota(jnp.int32, shape, axis)


def nt_dot(a, b):
    return lax.dot_general(a, b, (((1,), (1,)), ((), ())), preferred_element_type=F32)


def dot(a, b):
    return jnp.dot(a, b, preferred_element_type=F32)


def whole_kernel(
    density,
    kernel,
    electrode,
    drift_sign,
    taps,
    out,
    to_lines,
    lines,
    to_rows,
    rows,
    stage,
    half,
    double,
    drift,
    toeplitz,
    kick,
    offsets,
    send,
    recv,
):
    gx = lax.axis_index("gx")
    gy = lax.axis_index("gy")
    d = gx * 4 + gy
    me = (gx // 8, lax.rem(gx, 4), lax.rem(gx // 4, 2) * 2 + gy // 2, lax.rem(gy, 2))

    barrier = pltpu.get_barrier_semaphore()

    def greet(a, b):
        pl.semaphore_signal(barrier, inc=1, device_id=(a, b), device_id_type=MESH)

    for_each_peer(me, greet)

    def row_tile(ref, a, b):
        return ref.at[pl.ds(pl.multiple_of(a * XB, XB), XB), pl.ds(pl.multiple_of(b * 128, 128), 128)]

    def send_to_lines(r):
        def push(a, b):
            pltpu.make_async_remote_copy(
                src_ref=to_lines.at[a * 4 + b],
                dst_ref=row_tile(lines.at[r], gx, gy),
                send_sem=send.at[2 * r],
                recv_sem=recv.at[2 * r],
                device_id=(a, b),
                device_id_type=MESH,
            ).start()

        for_each_peer(me, push)
        pltpu.make_async_copy(to_lines.at[d], row_tile(lines.at[r], gx, gy), recv.at[2 * r]).start()

    def send_to_rows(r):
        def push(a, b):
            pltpu.make_async_remote_copy(
                src_ref=row_tile(to_rows, a, b),
                dst_ref=rows.at[r, d],
                send_sem=send.at[2 * r + 1],
                recv_sem=recv.at[2 * r + 1],
                device_id=(a, b),
                device_id_type=MESH,
            ).start()

        for_each_peer(me, push)
        pltpu.make_async_copy(row_tile(to_rows, gx, gy), rows.at[r, d], recv.at[2 * r + 1]).start()

    def wait_lines(r):
        pltpu.make_async_copy(lines.at[r], lines.at[r], recv.at[2 * r]).wait()

    def wait_rows(r):
        pltpu.make_async_copy(rows.at[r], rows.at[r], recv.at[2 * r + 1]).wait()

    def wait_sent(s):
        sent = to_lines.at[pl.ds(0, PARTS - 1)]
        pltpu.make_async_copy(sent, sent, send.at[s]).wait()

    eye = (iota((128, 128), 0) == iota((128, 128), 1)).astype(BF16)

    def pack(x, carry):
        block = jnp.concatenate([density[x, :, 128 * j : 128 * j + 128] for j in range(4)], axis=0)
        stage[pl.ds(x, 128, stride=XB), :] = nt_dot(eye, block.astype(BF16))
        return carry

    lax.fori_loop(0, XB, pack, 0)
    to_lines[...] = stage[...].astype(BF16).reshape(PARTS, XB, 128)

    pl.semaphore_wait(barrier, PARTS - 1)
    send_to_lines(0)

    parity = lax.rem(d, 2)

    def circulant(row_even, row_odd, shift):
        row = jnp.where(parity == 0, row_even, row_odd)
        row = pltpu.roll(jnp.broadcast_to(row, (8, NX)), shift, 1)[0:1, :]
        wide = jnp.broadcast_to(row, (NX, NX))
        return pltpu.roll(wide, 0, 1, stride=1, stride_axis=0)

    half[...] = circulant(taps[0:1, :], taps[1:2, :], NX - 127 + d // 2).astype(BF16)
    double[...] = circulant(taps[2:3, :], taps[3:4, :], NX - 255 + d).astype(BF16)

    col = iota((16, 512), 1)
    col_y = (col // 128) * 32 + lax.rem(col, 32)
    col_p = lax.rem(col // 32, 4) * 128 + d
    speed = 0.5 * ((2 * col_p - (NP - 1)).astype(F32) / NP)

    def sign_at(cell):
        slab = cell // 16
        chosen = jnp.zeros((16, 512), jnp.int32)
        for s in range(8):
            chosen = jnp.where(slab == s, drift_sign[s], chosen)
        return (2 * chosen - 1).astype(F32)

    face_low = speed * sign_at(jnp.maximum(col_y - 1, 0))
    face_high = speed * sign_at(col_y)
    keep = 1.0 - jnp.maximum(face_high, 0.0) + jnp.minimum(face_low, 0.0)
    from_next = jnp.where(col_y == 127, 0.0, -jnp.minimum(face_high, 0.0))
    from_prev = jnp.where(col_y == 0, 0.0, jnp.maximum(face_low, 0.0))
    inner = lax.rem(col, 32)
    band = jnp.where(iota((16, 512), 0) == 8, 1.0, 0.0).astype(F32)
    for _ in range(4):
        after = jnp.where(inner == 31, pltpu.roll(band, 512 - 97, 1), pltpu.roll(band, 511, 1))
        before = jnp.where(inner == 0, pltpu.roll(band, 97, 1), pltpu.roll(band, 1, 1))
        band = (
            keep * band
            + from_next * pltpu.roll(after, 1, 0)
            + from_prev * pltpu.roll(before, 15, 0)
        )
    for b in range(4):
        row = iota((128, 512), 0)
        column = iota((128, 512), 1)
        gap = (b * 32 + lax.rem(row, 32)) - ((column // 128) * 32 + lax.rem(column, 32))
        gap = jnp.where(row // 32 == lax.rem(column // 32, 4), gap, 99)
        matrix = jnp.zeros((128, 512), F32)
        for step in range(-4, 5):
            matrix = jnp.where(gap == step, band[8 + step : 9 + step, :], matrix)
        drift[128 * b : 128 * b + 128, :] = matrix.astype(BF16)

    flip = (iota((512, 512), 0) == lax.rem(512 - iota((512, 512), 1), 512)).astype(BF16)
    forward = kernel[...].astype(F32)
    backward = dot(kernel[...], flip)
    ahead = jnp.where(iota((NV, 512), 1) == 0, forward, -forward)
    both = jnp.concatenate([ahead, backward], axis=1)
    for v in range(NV):
        offsets[v] = both[v : v + 1, :]

    lane_block = iota((128, 128), 1) // 32
    wide_block = lax.rem(iota((512, 512), 1) // 32, 4)

    def advect(r, matrix, with_drift, cells):
        if with_drift:
            current = dot(lines[r], drift[...]).astype(BF16)
        else:
            current = lines[r]
        turned = current
        for j in range(1, 4):
            cut = cells * j
            moved = jnp.concatenate([current[cut:], current[:cut]], axis=0)
            turned = jnp.where(wide_block == j, moved, turned)
        to_rows[...] = dot(matrix[...], turned).astype(BF16)

    spread = (
        iota((128, 512), 0) == (iota((128, 512), 1) // 128) * 32 + lax.rem(iota((128, 512), 1), 32)
    ).astype(BF16)

    def build_kicks():
        def build(x, carry):
            base = jnp.broadcast_to(offsets[electrode[x]], (128, 1024))
            base = pltpu.roll(base, 0, 1, stride=1, stride_axis=0).astype(BF16)
            for t in range(4):
                for c in range(4):
                    at = 128 * ((c - t) % 8)
                    toeplitz[128 * t : 128 * t + 128, 128 * c : 128 * c + 128] = base[:, at : at + 128]
            square = dot(toeplitz[...], toeplitz[...])
            kick[x] = (toeplitz[...].astype(F32) + 0.5 * square).astype(BF16)
            return carry

        lax.fori_loop(0, XB, build, 0)

    def kick_rows(r):
        stage[...] = rows[r].reshape(PARTS * XB, 128).astype(F32)

        def one(x, carry):
            current = stage[pl.ds(x, 128, stride=XB), :]
            repeated = dot(current.astype(BF16), spread).astype(BF16)
            operand = jnp.concatenate([repeated[:, 128 * j : 128 * j + 128] for j in range(4)], axis=0)
            product = dot(kick[x], operand)
            change = product[0:128]
            for j in range(1, 4):
                change = jnp.where(lane_block == j, product[128 * j : 128 * j + 128], change)
            stage[pl.ds(x, 128, stride=XB), :] = current + change
            return carry

        lax.fori_loop(0, XB, one, 0)
        wait_sent(2 * r)
        to_lines[...] = stage[...].astype(BF16).reshape(PARTS, XB, 128)

    wait_lines(0)
    advect(0, half, True, 64)
    send_to_rows(0)
    build_kicks()
    wait_rows(0)
    kick_rows(0)
    send_to_lines(1)
    wait_lines(1)
    wait_sent(1)
    advect(1, double, True, 128)
    send_to_rows(1)
    wait_rows(1)
    kick_rows(1)
    send_to_lines(2)
    wait_lines(2)
    wait_sent(3)
    advect(2, half, False, 64)
    send_to_rows(2)
    wait_rows(2)
    stage[...] = rows[2].reshape(PARTS * XB, 128).astype(F32)

    def unpack(x, carry):
        current = stage[pl.ds(x, 128, stride=XB), :].astype(BF16)
        turned = nt_dot(eye, current)
        for j in range(4):
            out[x, :, 128 * j : 128 * j + 128] = turned[32 * j : 32 * j + 32, :]
        return carry

    lax.fori_loop(0, XB, unpack, 0)
    wait_sent(4)
    wait_sent(5)


def on_device(density, kernel, electrode, drift_sign):
    vmem = pl.BlockSpec(memory_space=pltpu.VMEM)
    smem = pl.BlockSpec(memory_space=pltpu.SMEM)
    return pl.pallas_call(
        whole_kernel,
        out_shape=jax.ShapeDtypeStruct(density.shape, F32),
        in_specs=[vmem, vmem, smem, smem, vmem],
        out_specs=vmem,
        scratch_shapes=[
            pltpu.VMEM((PARTS, XB, 128), BF16),
            pltpu.VMEM((3, NX, 512), BF16),
            pltpu.VMEM((NX, 512), BF16),
            pltpu.VMEM((3, PARTS, XB, 128), BF16),
            pltpu.VMEM((PARTS * XB, 128), F32),
            pltpu.VMEM((NX, NX), BF16),
            pltpu.VMEM((NX, NX), BF16),
            pltpu.VMEM((512, 512), BF16),
            pltpu.VMEM((NP, NP), BF16),
            pltpu.VMEM((XB, NP, NP), BF16),
            pltpu.VMEM((NV, 1, 1024), F32),
            pltpu.SemaphoreType.DMA((6,)),
            pltpu.SemaphoreType.DMA((6,)),
        ],
        compiler_params=pltpu.CompilerParams(
            collective_id=0, has_side_effects=True, vmem_limit_bytes=56 << 20
        ),
    )(density, kernel, electrode, drift_sign, jnp.asarray(shift_kernels()))


def solution(mesh):
    return jax.shard_map(
        on_device,
        mesh=mesh,
        in_specs=(P("gx", "gy", None), P(), P("gx"), P()),
        out_specs=P("gx", "gy", None),
        check_vma=False,
    )
```

```python
import functools

import jax
import jax.numpy as jnp
import numpy as np
from jax import lax
from jax.experimental import pallas as pl
from jax.experimental.pallas import tpu as pltpu
from jax.sharding import PartitionSpec as P

NX = 512
NP = 512
XB = 16
YB = 32
NV = 16
PARTS = 128
MESH = pl.DeviceIdType.MESH
F32 = jnp.float32
BF16 = jnp.bfloat16


def shift_kernels():
    k = np.arange(NX)
    kappa = np.where(k > NX // 2, k - NX, k).astype(np.int64)
    n = np.arange(NX)
    rows = np.zeros((8, NX), np.float64)
    for parity in range(2):
        p = parity
        m = (kappa * (NX // 4) * (NP - 1 - 2 * p)) % (NX * NP)
        phase = 2 * np.pi * m / (NX * NP)
        g = np.cos(2 * np.pi * ((n[:, None] * k[None, :]) % NX) / NX - phase[None, :]).sum(1) / NX
        spectrum = np.fft.fft(g)
        g2 = np.fft.ifft(spectrum * spectrum).real
        whole = 127 - p // 2
        whole2 = 255 - p
        rows[parity] = np.roll(g, -whole)[(-n) % NX]
        rows[2 + parity] = np.roll(g2, -whole2)[(-n) % NX]
    return rows.astype(np.float32)


def send_order():
    ring = lambda t: min(t, 4 - t)
    offsets = [o for o in range(64)]
    key = lambda o: -(ring(o // 16) + ring(o // 4 % 4) + ring(o % 4))
    offsets.sort(key=lambda o: (key(o), (o * 37) % 64))
    offsets = offsets[:63]
    packed = []
    for i in range(0, 63, 3):
        trio = offsets[i : i + 3]
        packed.append(trio[0] + 64 * trio[1] + 4096 * trio[2])
    return packed


ORDER = send_order()


def for_each_peer(me, visit):
    y, z, x, core = me

    def group(g, carry):
        code = jnp.int32(0)
        for i, value in enumerate(ORDER):
            code = jnp.where(g == i, jnp.int32(value), code)

        def one(_, code):
            o = lax.rem(code, 64)
            y2 = lax.rem(y + o // 16, 4)
            z2 = lax.rem(z + lax.rem(o // 4, 4), 4)
            x2 = lax.rem(x + lax.rem(o, 4), 4)
            gx = y2 * 8 + (x2 // 2) * 4 + z2
            gy = lax.rem(x2, 2) * 2
            visit(gx, gy)
            visit(gx, gy + 1)
            return code // 64

        lax.fori_loop(0, 3, one, code)
        return carry

    lax.fori_loop(0, len(ORDER), group, 0)
    gx = y * 8 + (x // 2) * 4 + z
    visit(gx, lax.rem(x, 2) * 2 + 1 - core)


def iota(shape, axis):
    return lax.broadcasted_iota(jnp.int32, shape, axis)


def nt_dot(a, b):
    return lax.dot_general(a, b, (((1,), (1,)), ((), ())), preferred_element_type=F32)


def dot(a, b):
    return jnp.dot(a, b, preferred_element_type=F32)


def whole_kernel(
    density,
    kernel,
    electrode,
    drift_sign,
    taps,
    out,
    to_lines,
    lines,
    to_rows,
    rows,
    stage,
    half,
    double,
    drift,
    kicked,
    kick,
    offsets,
    send,
    recv,
):
    gx = lax.axis_index("gx")
    gy = lax.axis_index("gy")
    d = gx * 4 + gy
    me = (gx // 8, lax.rem(gx, 4), lax.rem(gx // 4, 2) * 2 + gy // 2, lax.rem(gy, 2))

    barrier = pltpu.get_barrier_semaphore()

    def greet(a, b):
        pl.semaphore_signal(barrier, inc=1, device_id=(a, b), device_id_type=MESH)

    for_each_peer(me, greet)

    def row_tile(ref, a, b):
        return ref.at[pl.ds(pl.multiple_of(a * XB, XB), XB), pl.ds(pl.multiple_of(b * 128, 128), 128)]

    def send_to_lines(r):
        def push(a, b):
            pltpu.make_async_remote_copy(
                src_ref=to_lines.at[a * 4 + b],
                dst_ref=row_tile(lines.at[r], gx, gy),
                send_sem=send.at[2 * r],
                recv_sem=recv.at[2 * r],
                device_id=(a, b),
                device_id_type=MESH,
            ).start()

        for_each_peer(me, push)
        pltpu.make_async_copy(to_lines.at[d], row_tile(lines.at[r], gx, gy), recv.at[2 * r]).start()

    def send_to_rows(r):
        def push(a, b):
            pltpu.make_async_remote_copy(
                src_ref=row_tile(to_rows, a, b),
                dst_ref=rows.at[r, d],
                send_sem=send.at[2 * r + 1],
                recv_sem=recv.at[2 * r + 1],
                device_id=(a, b),
                device_id_type=MESH,
            ).start()

        for_each_peer(me, push)
        pltpu.make_async_copy(row_tile(to_rows, gx, gy), rows.at[r, d], recv.at[2 * r + 1]).start()

    def wait_lines(r):
        pltpu.make_async_copy(lines.at[r], lines.at[r], recv.at[2 * r]).wait()

    def wait_rows(r):
        pltpu.make_async_copy(rows.at[r], rows.at[r], recv.at[2 * r + 1]).wait()

    def wait_sent(s):
        sent = to_lines.at[pl.ds(0, PARTS - 1)]
        pltpu.make_async_copy(sent, sent, send.at[s]).wait()

    eye = (iota((128, 128), 0) == iota((128, 128), 1)).astype(BF16)

    for x in range(XB):
        block = jnp.concatenate([density[x, :, 128 * j : 128 * j + 128] for j in range(4)], axis=0)
        stage[pl.ds(x, 128, stride=XB), :] = nt_dot(eye, block.astype(BF16))
    to_lines[...] = stage[...].astype(BF16).reshape(PARTS, XB, 128)

    flip = (iota((512, 512), 0) == lax.rem(512 - iota((512, 512), 1), 512)).astype(BF16)
    forward = kernel[...].astype(F32)
    backward = dot(kernel[...], flip)
    ahead = jnp.where(iota((NV, 512), 1) == 0, forward, -forward)
    both = jnp.concatenate([ahead, backward], axis=1)
    for v in range(NV):
        offsets[v] = both[v : v + 1, :]

    def build_kicks(start, stop):
        for x in range(start, stop):
            base = jnp.broadcast_to(offsets[electrode[x]], (128, 1024))
            base = pltpu.roll(base, 0, 1, stride=1, stride_axis=0).astype(BF16)
            shifted = [base[:, 128 * c : 128 * c + 128] for c in range(8)]
            matrix = jnp.concatenate(
                [jnp.concatenate([shifted[(c - t) % 8] for c in range(4)], axis=1) for t in range(4)],
                axis=0,
            )
            square = dot(matrix, matrix)
            for t in range(4):
                for c in range(4):
                    at = 128 * ((t - c) % 4)
                    kick[x, 128 * t : 128 * t + 128, at : at + 128] = (
                        shifted[(c - t) % 8].astype(F32)
                        + 0.5 * square[128 * t : 128 * t + 128, 128 * c : 128 * c + 128]
                    ).astype(BF16)

    build_kicks(0, 4)
    pl.semaphore_wait(barrier, PARTS - 1)
    send_to_lines(0)

    parity = lax.rem(d, 2)

    def circulant(row_even, row_odd, shift):
        row = jnp.where(parity == 0, row_even, row_odd)
        row = pltpu.roll(jnp.broadcast_to(row, (8, NX)), shift, 1)[0:1, :]
        wide = jnp.broadcast_to(row, (NX, NX))
        return pltpu.roll(wide, 0, 1, stride=1, stride_axis=0)

    half[...] = circulant(taps[0:1, :], taps[1:2, :], NX - 127 + d // 2).astype(BF16)
    double[...] = circulant(taps[2:3, :], taps[3:4, :], NX - 255 + d).astype(BF16)

    col = iota((16, 512), 1)
    col_y = (col // 128) * 32 + lax.rem(col, 32)
    col_p = lax.rem(col // 32, 4) * 128 + d
    speed = 0.5 * ((2 * col_p - (NP - 1)).astype(F32) / NP)

    def sign_at(cell):
        slab = cell // 16
        chosen = jnp.zeros((16, 512), jnp.int32)
        for s in range(8):
            chosen = jnp.where(slab == s, drift_sign[s], chosen)
        return (2 * chosen - 1).astype(F32)

    face_low = speed * sign_at(jnp.maximum(col_y - 1, 0))
    face_high = speed * sign_at(col_y)
    keep = 1.0 - jnp.maximum(face_high, 0.0) + jnp.minimum(face_low, 0.0)
    from_next = jnp.where(col_y == 127, 0.0, -jnp.minimum(face_high, 0.0))
    from_prev = jnp.where(col_y == 0, 0.0, jnp.maximum(face_low, 0.0))
    inner = lax.rem(col, 32)
    band = jnp.where(iota((16, 512), 0) == 8, 1.0, 0.0).astype(F32)
    for _ in range(4):
        after = jnp.where(inner == 31, pltpu.roll(band, 512 - 97, 1), pltpu.roll(band, 511, 1))
        before = jnp.where(inner == 0, pltpu.roll(band, 97, 1), pltpu.roll(band, 1, 1))
        band = (
            keep * band
            + from_next * pltpu.roll(after, 1, 0)
            + from_prev * pltpu.roll(before, 15, 0)
        )
    for b in range(4):
        row = iota((128, 512), 0)
        column = iota((128, 512), 1)
        gap = (b * 32 + lax.rem(row, 32)) - ((column // 128) * 32 + lax.rem(column, 32))
        gap = jnp.where(row // 32 == lax.rem(column // 32, 4), gap, 99)
        matrix = jnp.zeros((128, 512), F32)
        for step in range(-4, 5):
            matrix = jnp.where(gap == step, band[8 + step : 9 + step, :], matrix)
        drift[128 * b : 128 * b + 128, :] = matrix.astype(BF16)

    lane_block = iota((128, 128), 1) // 32
    wide_block = lax.rem(iota((512, 512), 1) // 32, 4)

    def advect(r, matrix, with_drift, cells):
        if with_drift:
            current = dot(lines[r], drift[...]).astype(BF16)
        else:
            current = lines[r]
        turned = current
        for j in range(1, 4):
            cut = cells * j
            moved = jnp.concatenate([current[cut:], current[:cut]], axis=0)
            turned = jnp.where(wide_block == j, moved, turned)
        to_rows[...] = dot(matrix[...], turned).astype(BF16)

    def kick_rows(r):
        stage[...] = rows[r].reshape(PARTS * XB, 128).astype(F32)
        for start in range(0, XB, 4):
            group = range(start, start + 4)
            current = [stage[pl.ds(x, 128, stride=XB), :] for x in group]
            operand = [
                jnp.concatenate([c] + [pltpu.roll(c, 32 * k, 1) for k in range(1, 4)], axis=0).astype(BF16)
                for c in current
            ]
            product = [dot(kick[x], o) for x, o in zip(group, operand)]
            for x, c, q in zip(group, current, product):
                change = q[0:128]
                for j in range(1, 4):
                    change = jnp.where(lane_block == j, q[128 * j : 128 * j + 128], change)
                kicked[pl.ds(x, 128, stride=XB), :] = c + change
        wait_sent(2 * r)
        to_lines[...] = kicked[...].astype(BF16).reshape(PARTS, XB, 128)

    build_kicks(4, 10)
    wait_lines(0)
    advect(0, half, True, 64)
    send_to_rows(0)
    build_kicks(10, 16)
    wait_rows(0)
    kick_rows(0)
    send_to_lines(1)
    wait_lines(1)
    wait_sent(1)
    advect(1, double, True, 128)
    send_to_rows(1)
    wait_rows(1)
    kick_rows(1)
    send_to_lines(2)
    wait_lines(2)
    wait_sent(3)
    advect(2, half, False, 64)
    send_to_rows(2)
    wait_rows(2)
    stage[...] = rows[2].reshape(PARTS * XB, 128).astype(F32)

    for x in range(XB):
        current = stage[pl.ds(x, 128, stride=XB), :].astype(BF16)
        turned = nt_dot(eye, current).astype(BF16)
        for j in range(4):
            out[x, :, 128 * j : 128 * j + 128] = turned[32 * j : 32 * j + 32, :]
    wait_sent(4)
    wait_sent(5)


def on_device(density, kernel, electrode, drift_sign):
    vmem = pl.BlockSpec(memory_space=pltpu.VMEM)
    smem = pl.BlockSpec(memory_space=pltpu.SMEM)
    final = pl.pallas_call(
        whole_kernel,
        out_shape=jax.ShapeDtypeStruct(density.shape, BF16),
        in_specs=[vmem, vmem, smem, smem, vmem],
        out_specs=vmem,
        scratch_shapes=[
            pltpu.VMEM((PARTS, XB, 128), BF16),
            pltpu.VMEM((3, NX, 512), BF16),
            pltpu.VMEM((NX, 512), BF16),
            pltpu.VMEM((3, PARTS, XB, 128), BF16),
            pltpu.VMEM((PARTS * XB, 128), F32),
            pltpu.VMEM((NX, NX), BF16),
            pltpu.VMEM((NX, NX), BF16),
            pltpu.VMEM((512, 512), BF16),
            pltpu.VMEM((PARTS * XB, 128), F32),
            pltpu.VMEM((XB, NP, NP), BF16),
            pltpu.VMEM((NV, 1, 1024), F32),
            pltpu.SemaphoreType.DMA((6,)),
            pltpu.SemaphoreType.DMA((6,)),
        ],
        compiler_params=pltpu.CompilerParams(
            collective_id=0, has_side_effects=True, vmem_limit_bytes=56 << 20
        ),
    )(density, kernel, electrode, drift_sign, jnp.asarray(shift_kernels()))
    return final.astype(F32)


def solution(mesh):
    return jax.shard_map(
        on_device,
        mesh=mesh,
        in_specs=(P("gx", "gy", None), P(), P("gx"), P()),
        out_specs=P("gx", "gy", None),
        check_vma=False,
    )
```

```python
import functools

import jax
import jax.numpy as jnp
import numpy as np
from jax import lax
from jax.experimental import pallas as pl
from jax.experimental.pallas import tpu as pltpu
from jax.sharding import PartitionSpec as P

NX = 512
NP = 512
XB = 16
YB = 32
NV = 16
PARTS = 128
MESH = pl.DeviceIdType.MESH
F32 = jnp.float32
BF16 = jnp.bfloat16


def shift_kernels():
    k = np.arange(NX)
    kappa = np.where(k > NX // 2, k - NX, k).astype(np.int64)
    n = np.arange(NX)
    rows = np.zeros((8, NX), np.float64)
    for parity in range(2):
        p = parity
        m = (kappa * (NX // 4) * (NP - 1 - 2 * p)) % (NX * NP)
        phase = 2 * np.pi * m / (NX * NP)
        g = np.cos(2 * np.pi * ((n[:, None] * k[None, :]) % NX) / NX - phase[None, :]).sum(1) / NX
        spectrum = np.fft.fft(g)
        g2 = np.fft.ifft(spectrum * spectrum).real
        whole = 127 - p // 2
        whole2 = 255 - p
        rows[parity] = np.roll(g, -whole)[(-n) % NX]
        rows[2 + parity] = np.roll(g2, -whole2)[(-n) % NX]
    return rows.astype(np.float32)


def send_order():
    ring = lambda t: min(t, 4 - t)
    far = lambda o: ring(o // 16) + ring(o // 4 % 4) + ring(o % 4)
    return sorted(range(1, 64), key=lambda o: (-far(o), (o * 37) % 64))


ORDER = send_order()


def peers(me):
    y, z, x, core = me
    ys = [lax.rem(y + i, 4) * 8 for i in range(4)]
    zs = [lax.rem(z + i, 4) for i in range(4)]
    xs = [lax.rem(x + i, 4) for i in range(4)]
    high = [t // 2 * 4 for t in xs]
    low = [lax.rem(t, 2) * 2 for t in xs]
    everyone, column = [], []
    for o in ORDER:
        gx = ys[o // 16] + zs[o // 4 % 4] + high[o % 4]
        gy = low[o % 4]
        everyone += [(gx, gy), (gx, gy + 1)]
        if o % 2 == 0:
            column.append(gx)
    everyone.append((ys[0] + zs[0] + high[0], low[0] + 1 - core))
    return everyone, column


def iota(shape, axis):
    return lax.broadcasted_iota(jnp.int32, shape, axis)


def nt_dot(a, b):
    return lax.dot_general(a, b, (((1,), (1,)), ((), ())), preferred_element_type=F32)


def dot(a, b):
    return jnp.dot(a, b, preferred_element_type=F32)


def whole_kernel(
    density,
    kernel,
    electrode,
    drift_sign,
    taps,
    out,
    to_lines,
    lines,
    to_rows,
    rows,
    stage,
    last_lines,
    last_out,
    last_rows,
    half,
    double,
    last,
    drift,
    kicked,
    kick,
    offsets,
    send,
    recv,
):
    gx = lax.axis_index("gx")
    gy = lax.axis_index("gy")
    d = gx * 4 + gy
    me = (gx // 8, lax.rem(gx, 4), lax.rem(gx // 4, 2) * 2 + gy // 2, lax.rem(gy, 2))

    everyone, same_gy = peers(me)

    barrier = pltpu.get_barrier_semaphore()
    for peer in everyone:
        pl.semaphore_signal(barrier, inc=1, device_id=peer, device_id_type=MESH)

    def row_tile(ref, a, b):
        return ref.at[pl.ds(pl.multiple_of(a * XB, XB), XB), pl.ds(pl.multiple_of(b * 128, 128), 128)]

    def send_to_lines(r):
        for a, b in everyone:
            pltpu.make_async_remote_copy(
                src_ref=to_lines.at[a * 4 + b],
                dst_ref=row_tile(lines.at[r], gx, gy),
                send_sem=send.at[2 * r],
                recv_sem=recv.at[2 * r],
                device_id=(a, b),
                device_id_type=MESH,
            ).start()
        pltpu.make_async_copy(to_lines.at[d], row_tile(lines.at[r], gx, gy), recv.at[2 * r]).start()

    def send_to_rows(r):
        for a, b in everyone:
            pltpu.make_async_remote_copy(
                src_ref=row_tile(to_rows, a, b),
                dst_ref=rows.at[r, d],
                send_sem=send.at[2 * r + 1],
                recv_sem=recv.at[2 * r + 1],
                device_id=(a, b),
                device_id_type=MESH,
            ).start()
        pltpu.make_async_copy(row_tile(to_rows, gx, gy), rows.at[r, d], recv.at[2 * r + 1]).start()

    def slab(ref, a):
        return ref.at[:, pl.ds(pl.multiple_of(a * XB, XB), XB), :]

    def fan(ref, a):
        return ref.at[:, a]

    def send_last_lines():
        source = to_lines.reshape(4, 32, XB, 128)
        for a in same_gy:
            pltpu.make_async_remote_copy(
                src_ref=fan(source, a),
                dst_ref=slab(last_lines, gx),
                send_sem=send.at[4],
                recv_sem=recv.at[4],
                device_id=(a, gy),
                device_id_type=MESH,
            ).start()
        pltpu.make_async_copy(fan(source, gx), slab(last_lines, gx), recv.at[4]).start()

    def send_last_rows():
        target = last_rows.reshape(4, 32, XB, 128)
        for a in same_gy:
            pltpu.make_async_remote_copy(
                src_ref=slab(last_out, a),
                dst_ref=fan(target, gx),
                send_sem=send.at[5],
                recv_sem=recv.at[5],
                device_id=(a, gy),
                device_id_type=MESH,
            ).start()
        pltpu.make_async_copy(slab(last_out, gx), fan(target, gx), recv.at[5]).start()

    def wait_lines(r):
        pltpu.make_async_copy(lines.at[r], lines.at[r], recv.at[2 * r]).wait()

    def wait_rows(r):
        pltpu.make_async_copy(rows.at[r], rows.at[r], recv.at[2 * r + 1]).wait()

    def wait_sent(s, tiles=PARTS - 1):
        sent = to_lines.at[pl.ds(0, tiles)]
        pltpu.make_async_copy(sent, sent, send.at[s]).wait()

    eye = (iota((128, 128), 0) == iota((128, 128), 1)).astype(BF16)

    for x in range(XB):
        block = jnp.concatenate([density[x, :, 128 * j : 128 * j + 128] for j in range(4)], axis=0)
        stage[pl.ds(x, 128, stride=XB), :] = nt_dot(eye, block.astype(BF16))
    to_lines[...] = stage[...].astype(BF16).reshape(PARTS, XB, 128)

    flip = (iota((512, 512), 0) == lax.rem(512 - iota((512, 512), 1), 512)).astype(BF16)
    forward = kernel[...].astype(F32)
    backward = dot(kernel[...], flip)
    ahead = jnp.where(iota((NV, 512), 1) == 0, forward, -forward)
    both = jnp.concatenate([ahead, backward], axis=1)
    for v in range(NV):
        offsets[v] = both[v : v + 1, :]

    def build_kicks(start, stop):
        for x in range(start, stop):
            base = jnp.broadcast_to(offsets[electrode[x]], (128, 1024))
            base = pltpu.roll(base, 0, 1, stride=1, stride_axis=0).astype(BF16)
            shifted = [base[:, 128 * c : 128 * c + 128] for c in range(8)]
            matrix = jnp.concatenate(
                [jnp.concatenate([shifted[(c - t) % 8] for c in range(4)], axis=1) for t in range(4)],
                axis=0,
            )
            square = dot(matrix, matrix)
            for t in range(4):
                for c in range(4):
                    at = 128 * ((t - c) % 4)
                    kick[x, 128 * t : 128 * t + 128, at : at + 128] = (
                        shifted[(c - t) % 8].astype(F32)
                        + 0.5 * square[128 * t : 128 * t + 128, 128 * c : 128 * c + 128]
                    ).astype(BF16)

    build_kicks(0, 4)
    pl.semaphore_wait(barrier, PARTS - 1)
    send_to_lines(0)

    parity = lax.rem(d, 2)

    def circulant(odd, row_even, row_odd, shift):
        row = jnp.where(odd == 0, row_even, row_odd)
        row = pltpu.roll(jnp.broadcast_to(row, (8, NX)), shift, 1)[0:1, :]
        wide = jnp.broadcast_to(row, (NX, NX))
        return pltpu.roll(wide, 0, 1, stride=1, stride_axis=0)

    half[...] = circulant(parity, taps[0:1, :], taps[1:2, :], NX - 127 + d // 2).astype(BF16)
    double[...] = circulant(parity, taps[2:3, :], taps[3:4, :], NX - 255 + d).astype(BF16)

    last[...] = circulant(lax.rem(gx, 2), taps[0:1, :], taps[1:2, :], NX - 127 + gx // 2).astype(BF16)

    col = iota((16, 512), 1)
    col_y = (col // 128) * 32 + lax.rem(col, 32)
    col_p = lax.rem(col // 32, 4) * 128 + d
    speed = 0.5 * ((2 * col_p - (NP - 1)).astype(F32) / NP)

    def sign_at(cell):
        slab = cell // 16
        chosen = jnp.zeros((16, 512), jnp.int32)
        for s in range(8):
            chosen = jnp.where(slab == s, drift_sign[s], chosen)
        return (2 * chosen - 1).astype(F32)

    face_low = speed * sign_at(jnp.maximum(col_y - 1, 0))
    face_high = speed * sign_at(col_y)
    keep = 1.0 - jnp.maximum(face_high, 0.0) + jnp.minimum(face_low, 0.0)
    from_next = jnp.where(col_y == 127, 0.0, -jnp.minimum(face_high, 0.0))
    from_prev = jnp.where(col_y == 0, 0.0, jnp.maximum(face_low, 0.0))
    inner = lax.rem(col, 32)
    band = jnp.where(iota((16, 512), 0) == 8, 1.0, 0.0).astype(F32)
    for _ in range(4):
        after = jnp.where(inner == 31, pltpu.roll(band, 512 - 97, 1), pltpu.roll(band, 511, 1))
        before = jnp.where(inner == 0, pltpu.roll(band, 97, 1), pltpu.roll(band, 1, 1))
        band = (
            keep * band
            + from_next * pltpu.roll(after, 1, 0)
            + from_prev * pltpu.roll(before, 15, 0)
        )
    for b in range(4):
        row = iota((128, 512), 0)
        column = iota((128, 512), 1)
        gap = (b * 32 + lax.rem(row, 32)) - ((column // 128) * 32 + lax.rem(column, 32))
        gap = jnp.where(row // 32 == lax.rem(column // 32, 4), gap, 99)
        matrix = jnp.zeros((128, 512), F32)
        for step in range(-4, 5):
            matrix = jnp.where(gap == step, band[8 + step : 9 + step, :], matrix)
        drift[128 * b : 128 * b + 128, :] = matrix.astype(BF16)

    lane_block = iota((128, 128), 1) // 32
    wide_block = lax.rem(iota((512, 512), 1) // 32, 4)

    def turn(current, block, cells):
        turned = current
        for j in range(4):
            cut = cells(j)
            moved = jnp.concatenate([current[cut:], current[:cut]], axis=0) if cut else current
            turned = jnp.where(block == j, moved, turned)
        return turned

    def advect(r, matrix, cells):
        current = dot(lines[r], drift[...]).astype(BF16)
        turned = turn(current, wide_block, lambda j: cells * j)
        to_rows[...] = dot(matrix[...], turned).astype(BF16)

    def advect_last():
        narrow = wide_block[:, :128]
        turned = [turn(last_lines[h], narrow, lambda j: 64 * j + 16 * h) for h in range(4)]
        result = dot(last[...], jnp.concatenate(turned, axis=1)).astype(BF16)
        for h in range(4):
            last_out[h] = result[:, 128 * h : 128 * h + 128]

    def kick_rows(r):
        stage[...] = rows[r].reshape(PARTS * XB, 128).astype(F32)
        for start in range(0, XB, 4):
            group = range(start, start + 4)
            current = [stage[pl.ds(x, 128, stride=XB), :] for x in group]
            operand = [
                jnp.concatenate([c] + [pltpu.roll(c, 32 * k, 1) for k in range(1, 4)], axis=0).astype(BF16)
                for c in current
            ]
            product = [dot(kick[x], o) for x, o in zip(group, operand)]
            for x, c, q in zip(group, current, product):
                change = q[0:128]
                for j in range(1, 4):
                    change = jnp.where(lane_block == j, q[128 * j : 128 * j + 128], change)
                kicked[pl.ds(x, 128, stride=XB), :] = c + change
        wait_sent(2 * r)
        to_lines[...] = kicked[...].astype(BF16).reshape(PARTS, XB, 128)

    build_kicks(4, 10)
    wait_lines(0)
    advect(0, half, 64)
    send_to_rows(0)
    build_kicks(10, 16)
    wait_rows(0)
    kick_rows(0)
    send_to_lines(1)
    wait_lines(1)
    wait_sent(1)
    advect(1, double, 128)
    send_to_rows(1)
    wait_rows(1)
    kick_rows(1)
    send_last_lines()
    pltpu.make_async_copy(last_lines, last_lines, recv.at[4]).wait()
    advect_last()
    send_last_rows()
    wait_sent(3)
    wait_sent(4, PARTS - 4)
    pltpu.make_async_copy(last_rows, last_rows, recv.at[5]).wait()
    stage[...] = last_rows[...].reshape(PARTS * XB, 128).astype(F32)
    for x in range(XB):
        current = stage[pl.ds(x, 128, stride=XB), :].astype(BF16)
        turned = nt_dot(eye, current).astype(BF16)
        for j in range(4):
            out[x, :, 128 * j : 128 * j + 128] = turned[32 * j : 32 * j + 32, :]
    wait_sent(5, PARTS - 4)


def on_device(density, kernel, electrode, drift_sign):
    vmem = pl.BlockSpec(memory_space=pltpu.VMEM)
    smem = pl.BlockSpec(memory_space=pltpu.SMEM)
    final = pl.pallas_call(
        whole_kernel,
        out_shape=jax.ShapeDtypeStruct(density.shape, BF16),
        in_specs=[vmem, vmem, smem, smem, vmem],
        out_specs=vmem,
        scratch_shapes=[
            pltpu.VMEM((PARTS, XB, 128), BF16),
            pltpu.VMEM((2, NX, 512), BF16),
            pltpu.VMEM((NX, 512), BF16),
            pltpu.VMEM((2, PARTS, XB, 128), BF16),
            pltpu.VMEM((PARTS * XB, 128), F32),
            pltpu.VMEM((4, NX, 128), BF16),
            pltpu.VMEM((4, NX, 128), BF16),
            pltpu.VMEM((PARTS, XB, 128), BF16),
            pltpu.VMEM((NX, NX), BF16),
            pltpu.VMEM((NX, NX), BF16),
            pltpu.VMEM((NX, NX), BF16),
            pltpu.VMEM((512, 512), BF16),
            pltpu.VMEM((PARTS * XB, 128), F32),
            pltpu.VMEM((XB, NP, NP), BF16),
            pltpu.VMEM((NV, 1, 1024), F32),
            pltpu.SemaphoreType.DMA((6,)),
            pltpu.SemaphoreType.DMA((6,)),
        ],
        compiler_params=pltpu.CompilerParams(
            collective_id=0, has_side_effects=True, vmem_limit_bytes=56 << 20
        ),
    )(density, kernel, electrode, drift_sign, jnp.asarray(shift_kernels()))
    return final.astype(F32)


def solution(mesh):
    return jax.shard_map(
        on_device,
        mesh=mesh,
        in_specs=(P("gx", "gy", None), P(), P("gx"), P()),
        out_specs=P("gx", "gy", None),
        check_vma=False,
    )
```

```python
import functools

import jax
import jax.numpy as jnp
import numpy as np
from jax import lax
from jax.experimental import pallas as pl
from jax.experimental.pallas import tpu as pltpu
from jax.sharding import PartitionSpec as P

NX = 512
NP = 512
XB = 16
YB = 32
NV = 16
PARTS = 128
MESH = pl.DeviceIdType.MESH
F32 = jnp.float32
BF16 = jnp.bfloat16


def shift_kernels():
    k = np.arange(NX)
    kappa = np.where(k > NX // 2, k - NX, k).astype(np.int64)
    n = np.arange(NX)
    rows = np.zeros((8, NX), np.float64)
    for parity in range(2):
        p = parity
        m = (kappa * (NX // 4) * (NP - 1 - 2 * p)) % (NX * NP)
        phase = 2 * np.pi * m / (NX * NP)
        g = np.cos(2 * np.pi * ((n[:, None] * k[None, :]) % NX) / NX - phase[None, :]).sum(1) / NX
        spectrum = np.fft.fft(g)
        g2 = np.fft.ifft(spectrum * spectrum).real
        whole = 127 - p // 2
        whole2 = 255 - p
        rows[parity] = np.roll(g, -whole)[(-n) % NX]
        rows[2 + parity] = np.roll(g2, -whole2)[(-n) % NX]
    return rows.astype(np.float32)


def send_order():
    ring = lambda t: min(t, 4 - t)
    far = lambda o: ring(o // 16) + ring(o // 4 % 4) + ring(o % 4)
    return sorted(range(1, 64), key=lambda o: (-far(o), (o * 37) % 64))


ORDER = send_order()


def peers(me):
    y, z, x, core = me
    across = lax.rem(y + 2, 4)
    mate = lambda t: t + 1 - 2 * lax.rem(t, 2)
    ys = [8 * t for t in (y, mate(across), across, mate(y))]
    zs = [lax.rem(z + i, 4) for i in range(4)]
    xs = [lax.rem(x + i, 4) for i in range(4)]
    high = [t // 2 * 4 for t in xs]
    low = [lax.rem(t, 2) * 2 for t in xs]
    everyone, column = [], []
    parts = ([], []), ([], [])
    for o in ORDER:
        gx = ys[o // 16] + zs[o // 4 % 4] + high[o % 4]
        gy = low[o % 4]
        part, part_column = parts[0 if o // 16 in (1, 2) else 1]
        pair = [(gx, gy), (gx, gy + 1)]
        everyone += pair
        part += pair
        if o % 2 == 0:
            column.append(gx)
            part_column.append(gx)
    sibling = (ys[0] + zs[0] + high[0], low[0] + 1 - core)
    everyone.append(sibling)
    parts[1][0].append(sibling)
    return everyone, column, parts


def iota(shape, axis):
    return lax.broadcasted_iota(jnp.int32, shape, axis)


def nt_dot(a, b):
    return lax.dot_general(a, b, (((1,), (1,)), ((), ())), preferred_element_type=F32)


def dot(a, b):
    return jnp.dot(a, b, preferred_element_type=F32)


def whole_kernel(
    density,
    kernel,
    electrode,
    drift_sign,
    taps,
    out,
    to_lines,
    lines,
    to_rows,
    rows,
    stage,
    last_lines,
    last_out,
    last_rows,
    half,
    double,
    last,
    drift,
    kicked,
    operands,
    kick,
    offsets,
    send,
    recv,
):
    gx = lax.axis_index("gx")
    gy = lax.axis_index("gy")
    d = gx * 4 + gy
    me = (gx // 8, lax.rem(gx, 4), lax.rem(gx // 4, 2) * 2 + gy // 2, lax.rem(gy, 2))

    everyone, same_gy, ((far, far_gy), (near, near_gy)) = peers(me)
    near_pair = me[0] // 2
    far_pair = 1 - near_pair

    barrier = pltpu.get_barrier_semaphore()
    for peer in everyone:
        pl.semaphore_signal(barrier, inc=1, device_id=peer, device_id_type=MESH)

    def row_tile(ref, a, b):
        return ref.at[pl.ds(pl.multiple_of(a * XB, XB), XB), pl.ds(pl.multiple_of(b * 128, 128), 128)]

    def send_to_lines(r, group):
        for a, b in group:
            pltpu.make_async_remote_copy(
                src_ref=to_lines.at[a * 4 + b],
                dst_ref=row_tile(lines.at[r], gx, gy),
                send_sem=send.at[2 * r],
                recv_sem=recv.at[2 * r],
                device_id=(a, b),
                device_id_type=MESH,
            ).start()

    def keep_lines(r):
        pltpu.make_async_copy(to_lines.at[d], row_tile(lines.at[r], gx, gy), recv.at[2 * r]).start()

    def send_to_rows(r, group):
        for a, b in group:
            pltpu.make_async_remote_copy(
                src_ref=row_tile(to_rows, a, b),
                dst_ref=rows.at[r, d],
                send_sem=send.at[2 * r + 1],
                recv_sem=recv.at[2 * r + 1],
                device_id=(a, b),
                device_id_type=MESH,
            ).start()

    def keep_rows(r):
        pltpu.make_async_copy(row_tile(to_rows, gx, gy), rows.at[r, d], recv.at[2 * r + 1]).start()

    def slab(ref, a):
        return ref.at[:, pl.ds(pl.multiple_of(a * XB, XB), XB), :]

    def fan(ref, a):
        return ref.at[:, a]

    def send_last_lines(group):
        source = to_lines.reshape(4, 32, XB, 128)
        for a in group:
            pltpu.make_async_remote_copy(
                src_ref=fan(source, a),
                dst_ref=slab(last_lines, gx),
                send_sem=send.at[4],
                recv_sem=recv.at[4],
                device_id=(a, gy),
                device_id_type=MESH,
            ).start()

    def keep_last_lines():
        source = to_lines.reshape(4, 32, XB, 128)
        pltpu.make_async_copy(fan(source, gx), slab(last_lines, gx), recv.at[4]).start()

    def send_last_rows(group):
        target = last_rows.reshape(4, 32, XB, 128)
        for a in group:
            pltpu.make_async_remote_copy(
                src_ref=slab(last_out, a),
                dst_ref=fan(target, gx),
                send_sem=send.at[5],
                recv_sem=recv.at[5],
                device_id=(a, gy),
                device_id_type=MESH,
            ).start()

    def keep_last_rows():
        target = last_rows.reshape(4, 32, XB, 128)
        pltpu.make_async_copy(slab(last_out, gx), fan(target, gx), recv.at[5]).start()

    def wait_lines(r):
        pltpu.make_async_copy(lines.at[r], lines.at[r], recv.at[2 * r]).wait()

    def wait_rows(r):
        pltpu.make_async_copy(rows.at[r], rows.at[r], recv.at[2 * r + 1]).wait()

    def wait_sent(s, tiles=PARTS - 1):
        sent = to_lines.at[pl.ds(0, tiles)]
        pltpu.make_async_copy(sent, sent, send.at[s]).wait()

    eye = (iota((128, 128), 0) == iota((128, 128), 1)).astype(BF16)

    for x in range(XB):
        block = jnp.concatenate([density[x, :, 128 * j : 128 * j + 128] for j in range(4)], axis=0)
        stage[pl.ds(x, 128, stride=XB), :] = nt_dot(eye, block.astype(BF16))
    to_lines[...] = stage[...].astype(BF16).reshape(PARTS, XB, 128)

    flip = (iota((512, 512), 0) == lax.rem(512 - iota((512, 512), 1), 512)).astype(BF16)
    forward = kernel[...].astype(F32)
    backward = dot(kernel[...], flip)
    ahead = jnp.where(iota((NV, 512), 1) == 0, forward, -forward)
    both = jnp.concatenate([ahead, backward], axis=1)
    for v in range(NV):
        offsets[v] = both[v : v + 1, :]

    def build_kicks(start, stop):
        for x in range(start, stop):
            base = jnp.broadcast_to(offsets[electrode[x]], (128, 1024))
            base = pltpu.roll(base, 0, 1, stride=1, stride_axis=0).astype(BF16)
            shifted = [base[:, 128 * c : 128 * c + 128] for c in range(8)]
            matrix = jnp.concatenate(
                [jnp.concatenate([shifted[(c - t) % 8] for c in range(4)], axis=1) for t in range(4)],
                axis=0,
            )
            square = dot(matrix, matrix)
            for t in range(4):
                for c in range(4):
                    at = 128 * ((t - c) % 4)
                    kick[x, 128 * t : 128 * t + 128, at : at + 128] = (
                        shifted[(c - t) % 8].astype(F32)
                        + 0.5 * square[128 * t : 128 * t + 128, 128 * c : 128 * c + 128]
                    ).astype(BF16)

    build_kicks(0, 4)
    pl.semaphore_wait(barrier, PARTS - 1)
    send_to_lines(0, everyone)
    keep_lines(0)

    parity = lax.rem(d, 2)

    def circulant(odd, row_even, row_odd, shift):
        row = jnp.where(odd == 0, row_even, row_odd)
        row = pltpu.roll(jnp.broadcast_to(row, (8, NX)), shift, 1)[0:1, :]
        wide = jnp.broadcast_to(row, (NX, NX))
        return pltpu.roll(wide, 0, 1, stride=1, stride_axis=0)

    half[...] = circulant(parity, taps[0:1, :], taps[1:2, :], NX - 127 + d // 2).astype(BF16)
    double[...] = circulant(parity, taps[2:3, :], taps[3:4, :], NX - 255 + d).astype(BF16)

    last[...] = circulant(lax.rem(gx, 2), taps[0:1, :], taps[1:2, :], NX - 127 + gx // 2).astype(BF16)

    col = iota((16, 512), 1)
    col_y = (col // 128) * 32 + lax.rem(col, 32)
    col_p = lax.rem(col // 32, 4) * 128 + d
    speed = 0.5 * ((2 * col_p - (NP - 1)).astype(F32) / NP)

    def sign_at(cell):
        slab = cell // 16
        chosen = jnp.zeros((16, 512), jnp.int32)
        for s in range(8):
            chosen = jnp.where(slab == s, drift_sign[s], chosen)
        return (2 * chosen - 1).astype(F32)

    face_low = speed * sign_at(jnp.maximum(col_y - 1, 0))
    face_high = speed * sign_at(col_y)
    keep = 1.0 - jnp.maximum(face_high, 0.0) + jnp.minimum(face_low, 0.0)
    from_next = jnp.where(col_y == 127, 0.0, -jnp.minimum(face_high, 0.0))
    from_prev = jnp.where(col_y == 0, 0.0, jnp.maximum(face_low, 0.0))
    inner = lax.rem(col, 32)
    band = jnp.where(iota((16, 512), 0) == 8, 1.0, 0.0).astype(F32)
    for _ in range(4):
        after = jnp.where(inner == 31, pltpu.roll(band, 512 - 97, 1), pltpu.roll(band, 511, 1))
        before = jnp.where(inner == 0, pltpu.roll(band, 97, 1), pltpu.roll(band, 1, 1))
        band = (
            keep * band
            + from_next * pltpu.roll(after, 1, 0)
            + from_prev * pltpu.roll(before, 15, 0)
        )
    for b in range(4):
        row = iota((128, 512), 0)
        column = iota((128, 512), 1)
        gap = (b * 32 + lax.rem(row, 32)) - ((column // 128) * 32 + lax.rem(column, 32))
        gap = jnp.where(row // 32 == lax.rem(column // 32, 4), gap, 99)
        matrix = jnp.zeros((128, 512), F32)
        for step in range(-4, 5):
            matrix = jnp.where(gap == step, band[8 + step : 9 + step, :], matrix)
        drift[128 * b : 128 * b + 128, :] = matrix.astype(BF16)

    lane_block = iota((128, 128), 1) // 32
    wide_block = lax.rem(iota((512, 512), 1) // 32, 4)

    def turn(current, block, cells):
        turned = current
        for j in range(4):
            cut = cells(j)
            moved = jnp.concatenate([current[cut:], current[:cut]], axis=0) if cut else current
            turned = jnp.where(block == j, moved, turned)
        return turned

    def advect(r, matrix, cells):
        current = dot(lines[r], drift[...]).astype(BF16)
        turned = turn(current, wide_block, lambda j: cells * j)
        for pair, group in ((far_pair, far), (near_pair, near)):
            at = pl.ds(pl.multiple_of(256 * pair, 256), 256)
            to_rows[at, :] = dot(matrix[at, :], turned).astype(BF16)
            send_to_rows(r, group)
        keep_rows(r)

    def advect_last():
        narrow = wide_block[:, :128]
        turned = [turn(last_lines[h], narrow, lambda j: 64 * j + 16 * h) for h in range(4)]
        turned = jnp.concatenate(turned, axis=1)
        for pair, group in ((far_pair, far_gy), (near_pair, near_gy)):
            at = pl.ds(pl.multiple_of(256 * pair, 256), 256)
            result = dot(last[at, :], turned).astype(BF16)
            for h in range(4):
                last_out[h, at, :] = result[:, 128 * h : 128 * h + 128]
            send_last_rows(group)
        keep_last_rows()

    def kick_rows(r, pieces, sends, send_group, keep):
        stage[...] = rows[r].reshape(PARTS * XB, 128).astype(F32)
        wait_sent(2 * r)
        for part, pair in enumerate((far_pair, near_pair)):
            if part == 1:
                send_group(sends[0])
            runs = pieces(pair)
            total = sum(count for _, count in runs)
            for start in range(0, XB, 4):
                group = range(start, start + 4)
                if part == 0:
                    current = [stage[pl.ds(x, 128, stride=XB), :] for x in group]
                    for x, c in zip(group, current):
                        operands[x] = jnp.concatenate(
                            [c] + [pltpu.roll(c, 32 * k, 1) for k in range(1, 4)], axis=0
                        ).astype(BF16)
                product = []
                for x in group:
                    left = jnp.concatenate(
                        [
                            kick[x, pl.ds(pl.multiple_of(128 * j + first, 16), count), :]
                            for j in range(4)
                            for first, count in runs
                        ],
                        axis=0,
                    )
                    product.append(dot(left, operands[x]))
                for x, q in zip(group, product):
                    change = q[0:total]
                    for j in range(1, 4):
                        change = jnp.where(lane_block[0:total] == j, q[total * j : total * j + total], change)
                    done = 0
                    for first, count in runs:
                        at = pl.ds(XB * first + x, count, stride=XB)
                        kicked[at, :] = stage[at, :] + change[done : done + count]
                        done += count
            for first, count in runs:
                block = kicked[pl.ds(pl.multiple_of(XB * first, 256), XB * count), :]
                to_lines[pl.ds(first, count)] = block.astype(BF16).reshape(count, XB, 128)
        send_group(sends[1])
        keep()

    build_kicks(4, 10)
    wait_lines(0)
    advect(0, half, 64)
    build_kicks(10, 16)
    wait_rows(0)
    kick_rows(
        0,
        lambda pair: [(64 * pair, 64)],
        (far, near),
        lambda group: send_to_lines(1, group),
        lambda: keep_lines(1),
    )
    wait_lines(1)
    wait_sent(1)
    advect(1, double, 128)
    wait_rows(1)
    kick_rows(
        1,
        lambda pair: [(32 * h + 16 * pair, 16) for h in range(4)],
        (far_gy, near_gy),
        send_last_lines,
        keep_last_lines,
    )
    pltpu.make_async_copy(last_lines, last_lines, recv.at[4]).wait()
    advect_last()
    wait_sent(3)
    wait_sent(4, PARTS - 4)
    pltpu.make_async_copy(last_rows, last_rows, recv.at[5]).wait()
    stage[...] = last_rows[...].reshape(PARTS * XB, 128).astype(F32)
    for x in range(XB):
        current = stage[pl.ds(x, 128, stride=XB), :].astype(BF16)
        turned = nt_dot(eye, current).astype(BF16)
        for j in range(4):
            out[x, :, 128 * j : 128 * j + 128] = turned[32 * j : 32 * j + 32, :]
    wait_sent(5, PARTS - 4)


def on_device(density, kernel, electrode, drift_sign):
    vmem = pl.BlockSpec(memory_space=pltpu.VMEM)
    smem = pl.BlockSpec(memory_space=pltpu.SMEM)
    final = pl.pallas_call(
        whole_kernel,
        out_shape=jax.ShapeDtypeStruct(density.shape, BF16),
        in_specs=[vmem, vmem, smem, smem, vmem],
        out_specs=vmem,
        scratch_shapes=[
            pltpu.VMEM((PARTS, XB, 128), BF16),
            pltpu.VMEM((2, NX, 512), BF16),
            pltpu.VMEM((NX, 512), BF16),
            pltpu.VMEM((2, PARTS, XB, 128), BF16),
            pltpu.VMEM((PARTS * XB, 128), F32),
            pltpu.VMEM((4, NX, 128), BF16),
            pltpu.VMEM((4, NX, 128), BF16),
            pltpu.VMEM((PARTS, XB, 128), BF16),
            pltpu.VMEM((NX, NX), BF16),
            pltpu.VMEM((NX, NX), BF16),
            pltpu.VMEM((NX, NX), BF16),
            pltpu.VMEM((512, 512), BF16),
            pltpu.VMEM((PARTS * XB, 128), F32),
            pltpu.VMEM((XB, NP, 128), BF16),
            pltpu.VMEM((XB, NP, NP), BF16),
            pltpu.VMEM((NV, 1, 1024), F32),
            pltpu.SemaphoreType.DMA((6,)),
            pltpu.SemaphoreType.DMA((6,)),
        ],
        compiler_params=pltpu.CompilerParams(
            collective_id=0, has_side_effects=True, vmem_limit_bytes=56 << 20
        ),
    )(density, kernel, electrode, drift_sign, jnp.asarray(shift_kernels()))
    return final.astype(F32)


def solution(mesh):
    return jax.shard_map(
        on_device,
        mesh=mesh,
        in_specs=(P("gx", "gy", None), P(), P("gx"), P()),
        out_specs=P("gx", "gy", None),
        check_vma=False,
    )
```

```python
import functools

import jax
import jax.numpy as jnp
import numpy as np
from jax import lax
from jax.experimental import pallas as pl
from jax.experimental.pallas import tpu as pltpu
from jax.sharding import PartitionSpec as P

NX = 512
NP = 512
XB = 16
YB = 32
NV = 16
PARTS = 128
MESH = pl.DeviceIdType.MESH
F32 = jnp.float32
BF16 = jnp.bfloat16


def shift_kernels():
    k = np.arange(NX)
    kappa = np.where(k > NX // 2, k - NX, k).astype(np.int64)
    n = np.arange(NX)
    rows = np.zeros((8, NX), np.float64)
    for parity in range(2):
        p = parity
        m = (kappa * (NX // 4) * (NP - 1 - 2 * p)) % (NX * NP)
        phase = 2 * np.pi * m / (NX * NP)
        g = np.cos(2 * np.pi * ((n[:, None] * k[None, :]) % NX) / NX - phase[None, :]).sum(1) / NX
        spectrum = np.fft.fft(g)
        g2 = np.fft.ifft(spectrum * spectrum).real
        whole = 127 - p // 2
        whole2 = 255 - p
        rows[parity] = np.roll(g, -whole)[(-n) % NX]
        rows[2 + parity] = np.roll(g2, -whole2)[(-n) % NX]
    return rows.astype(np.float32)


def send_order():
    ring = lambda t: min(t, 4 - t)
    far = lambda o: ring(o // 16) + ring(o // 4 % 4) + ring(o % 4)
    return sorted(range(1, 64), key=lambda o: (-far(o), (o * 11) % 64))


ORDER = send_order()


def peers(me):
    y, z, x, core = me
    across = lax.rem(y + 2, 4)
    mate = lambda t: t + 1 - 2 * lax.rem(t, 2)
    ys = [8 * t for t in (y, mate(across), across, mate(y))]
    zs = [lax.rem(z + i, 4) for i in range(4)]
    xs = [lax.rem(x + i, 4) for i in range(4)]
    high = [t // 2 * 4 for t in xs]
    low = [lax.rem(t, 2) * 2 for t in xs]
    everyone, column = [], []
    parts = ([], []), ([], [])
    for o in ORDER:
        gx = ys[o // 16] + zs[o // 4 % 4] + high[o % 4]
        gy = low[o % 4]
        part, part_column = parts[0 if o // 16 in (1, 2) else 1]
        pair = [(gx, gy), (gx, gy + 1)]
        everyone += pair
        part += pair
        if o % 2 == 0:
            column.append(gx)
            part_column.append(gx)
    sibling = (ys[0] + zs[0] + high[0], low[0] + 1 - core)
    everyone.append(sibling)
    parts[1][0].append(sibling)
    return everyone, column, parts


def iota(shape, axis):
    return lax.broadcasted_iota(jnp.int32, shape, axis)


def nt_dot(a, b):
    return lax.dot_general(a, b, (((1,), (1,)), ((), ())), preferred_element_type=F32)


def dot(a, b):
    return jnp.dot(a, b, preferred_element_type=F32)


def whole_kernel(
    density,
    kernel,
    electrode,
    drift_sign,
    taps,
    out,
    to_lines,
    lines,
    to_rows,
    rows,
    stage,
    last_lines,
    last_out,
    last_rows,
    half,
    double,
    last,
    drift,
    kicked,
    operands,
    kick,
    offsets,
    send,
    recv,
):
    gx = lax.axis_index("gx")
    gy = lax.axis_index("gy")
    d = gx * 4 + gy
    me = (gx // 8, lax.rem(gx, 4), lax.rem(gx // 4, 2) * 2 + gy // 2, lax.rem(gy, 2))

    everyone, same_gy, ((far, far_gy), (near, near_gy)) = peers(me)
    near_pair = me[0] // 2
    far_pair = 1 - near_pair

    barrier = pltpu.get_barrier_semaphore()
    for peer in everyone:
        pl.semaphore_signal(barrier, inc=1, device_id=peer, device_id_type=MESH)

    def row_tile(ref, a, b):
        return ref.at[pl.ds(pl.multiple_of(a * XB, XB), XB), pl.ds(pl.multiple_of(b * 128, 128), 128)]

    def send_to_lines(r, group):
        for a, b in group:
            pltpu.make_async_remote_copy(
                src_ref=to_lines.at[a * 4 + b],
                dst_ref=row_tile(lines.at[r], gx, gy),
                send_sem=send.at[2 * r],
                recv_sem=recv.at[2 * r],
                device_id=(a, b),
                device_id_type=MESH,
            ).start()

    def keep_lines(r):
        pltpu.make_async_copy(to_lines.at[d], row_tile(lines.at[r], gx, gy), recv.at[2 * r]).start()

    def send_to_rows(r, group):
        for a, b in group:
            pltpu.make_async_remote_copy(
                src_ref=row_tile(to_rows, a, b),
                dst_ref=rows.at[r, d],
                send_sem=send.at[2 * r + 1],
                recv_sem=recv.at[2 * r + 1],
                device_id=(a, b),
                device_id_type=MESH,
            ).start()

    def keep_rows(r):
        pltpu.make_async_copy(row_tile(to_rows, gx, gy), rows.at[r, d], recv.at[2 * r + 1]).start()

    def slab(ref, a):
        return ref.at[:, pl.ds(pl.multiple_of(a * XB, XB), XB), :]

    def fan(ref, a):
        return ref.at[:, a]

    def send_last_lines(group):
        source = to_lines.reshape(4, 32, XB, 128)
        for a in group:
            pltpu.make_async_remote_copy(
                src_ref=fan(source, a),
                dst_ref=slab(last_lines, gx),
                send_sem=send.at[4],
                recv_sem=recv.at[4],
                device_id=(a, gy),
                device_id_type=MESH,
            ).start()

    def keep_last_lines():
        source = to_lines.reshape(4, 32, XB, 128)
        pltpu.make_async_copy(fan(source, gx), slab(last_lines, gx), recv.at[4]).start()

    def send_last_rows(group):
        target = last_rows.reshape(4, 32, XB, 128)
        for a in group:
            pltpu.make_async_remote_copy(
                src_ref=slab(last_out, a),
                dst_ref=fan(target, gx),
                send_sem=send.at[5],
                recv_sem=recv.at[5],
                device_id=(a, gy),
                device_id_type=MESH,
            ).start()

    def keep_last_rows():
        target = last_rows.reshape(4, 32, XB, 128)
        pltpu.make_async_copy(slab(last_out, gx), fan(target, gx), recv.at[5]).start()

    def wait_lines(r):
        pltpu.make_async_copy(lines.at[r], lines.at[r], recv.at[2 * r]).wait()

    def wait_rows(r):
        pltpu.make_async_copy(rows.at[r], rows.at[r], recv.at[2 * r + 1]).wait()

    def wait_sent(s, tiles=PARTS - 1):
        sent = to_lines.at[pl.ds(0, tiles)]
        pltpu.make_async_copy(sent, sent, send.at[s]).wait()

    eye = (iota((128, 128), 0) == iota((128, 128), 1)).astype(BF16)

    for x in range(XB):
        block = jnp.concatenate([density[x, :, 128 * j : 128 * j + 128] for j in range(4)], axis=0)
        stage[pl.ds(x, 128, stride=XB), :] = nt_dot(eye, block.astype(BF16))
    to_lines[...] = stage[...].astype(BF16).reshape(PARTS, XB, 128)

    flip = (iota((512, 512), 0) == lax.rem(512 - iota((512, 512), 1), 512)).astype(BF16)
    forward = kernel[...].astype(F32)
    backward = dot(kernel[...], flip)
    ahead = jnp.where(iota((NV, 512), 1) == 0, forward, -forward)
    both = jnp.concatenate([ahead, backward], axis=1)
    for v in range(NV):
        offsets[v] = both[v : v + 1, :]

    def build_kicks(start, stop):
        for x in range(start, stop):
            base = jnp.broadcast_to(offsets[electrode[x]], (128, 1024))
            base = pltpu.roll(base, 0, 1, stride=1, stride_axis=0).astype(BF16)
            shifted = [base[:, 128 * c : 128 * c + 128] for c in range(8)]
            matrix = jnp.concatenate(
                [jnp.concatenate([shifted[(c - t) % 8] for c in range(4)], axis=1) for t in range(4)],
                axis=0,
            )
            square = dot(matrix, matrix)
            for t in range(4):
                for c in range(4):
                    at = 128 * ((t - c) % 4)
                    kick[x, 128 * t : 128 * t + 128, at : at + 128] = (
                        shifted[(c - t) % 8].astype(F32)
                        + 0.5 * square[128 * t : 128 * t + 128, 128 * c : 128 * c + 128]
                    ).astype(BF16)

    build_kicks(0, 4)
    pl.semaphore_wait(barrier, PARTS - 1)
    send_to_lines(0, everyone)
    keep_lines(0)

    parity = lax.rem(d, 2)

    def circulant(odd, row_even, row_odd, shift):
        row = jnp.where(odd == 0, row_even, row_odd)
        row = pltpu.roll(jnp.broadcast_to(row, (8, NX)), shift, 1)[0:1, :]
        wide = jnp.broadcast_to(row, (NX, NX))
        return pltpu.roll(wide, 0, 1, stride=1, stride_axis=0)

    half[...] = circulant(parity, taps[0:1, :], taps[1:2, :], NX - 127 + d // 2).astype(BF16)
    double[...] = circulant(parity, taps[2:3, :], taps[3:4, :], NX - 255 + d).astype(BF16)

    last[...] = circulant(lax.rem(gx, 2), taps[0:1, :], taps[1:2, :], NX - 127 + gx // 2).astype(BF16)

    col = iota((16, 512), 1)
    col_y = (col // 128) * 32 + lax.rem(col, 32)
    col_p = lax.rem(col // 32, 4) * 128 + d
    speed = 0.5 * ((2 * col_p - (NP - 1)).astype(F32) / NP)

    def sign_at(cell):
        slab = cell // 16
        chosen = jnp.zeros((16, 512), jnp.int32)
        for s in range(8):
            chosen = jnp.where(slab == s, drift_sign[s], chosen)
        return (2 * chosen - 1).astype(F32)

    face_low = speed * sign_at(jnp.maximum(col_y - 1, 0))
    face_high = speed * sign_at(col_y)
    keep = 1.0 - jnp.maximum(face_high, 0.0) + jnp.minimum(face_low, 0.0)
    from_next = jnp.where(col_y == 127, 0.0, -jnp.minimum(face_high, 0.0))
    from_prev = jnp.where(col_y == 0, 0.0, jnp.maximum(face_low, 0.0))
    inner = lax.rem(col, 32)
    band = jnp.where(iota((16, 512), 0) == 8, 1.0, 0.0).astype(F32)
    for _ in range(4):
        after = jnp.where(inner == 31, pltpu.roll(band, 512 - 97, 1), pltpu.roll(band, 511, 1))
        before = jnp.where(inner == 0, pltpu.roll(band, 97, 1), pltpu.roll(band, 1, 1))
        band = (
            keep * band
            + from_next * pltpu.roll(after, 1, 0)
            + from_prev * pltpu.roll(before, 15, 0)
        )
    for b in range(4):
        row = iota((128, 512), 0)
        column = iota((128, 512), 1)
        gap = (b * 32 + lax.rem(row, 32)) - ((column // 128) * 32 + lax.rem(column, 32))
        gap = jnp.where(row // 32 == lax.rem(column // 32, 4), gap, 99)
        matrix = jnp.zeros((128, 512), F32)
        for step in range(-4, 5):
            matrix = jnp.where(gap == step, band[8 + step : 9 + step, :], matrix)
        drift[128 * b : 128 * b + 128, :] = matrix.astype(BF16)

    lane_block = iota((128, 128), 1) // 32
    wide_block = lax.rem(iota((512, 512), 1) // 32, 4)

    def turn(current, block, cells):
        turned = current
        for j in range(4):
            cut = cells(j)
            moved = jnp.concatenate([current[cut:], current[:cut]], axis=0) if cut else current
            turned = jnp.where(block == j, moved, turned)
        return turned

    def advect(r, matrix, cells):
        current = dot(lines[r], drift[...]).astype(BF16)
        turned = turn(current, wide_block, lambda j: cells * j)
        for pair, group in ((far_pair, far), (near_pair, near)):
            at = pl.ds(pl.multiple_of(256 * pair, 256), 256)
            to_rows[at, :] = dot(matrix[at, :], turned).astype(BF16)
            send_to_rows(r, group)
        keep_rows(r)

    def advect_last():
        narrow = wide_block[:, :128]
        turned = [turn(last_lines[h], narrow, lambda j: 64 * j + 16 * h) for h in range(4)]
        turned = jnp.concatenate(turned, axis=1)
        for pair, group in ((far_pair, far_gy), (near_pair, near_gy)):
            at = pl.ds(pl.multiple_of(256 * pair, 256), 256)
            result = dot(last[at, :], turned).astype(BF16)
            for h in range(4):
                last_out[h, at, :] = result[:, 128 * h : 128 * h + 128]
            send_last_rows(group)
        keep_last_rows()

    def kick_rows(r, pieces, sends, send_group, keep):
        stage[...] = rows[r].reshape(PARTS * XB, 128).astype(F32)
        wait_sent(2 * r)
        for part, pair in enumerate((far_pair, near_pair)):
            if part == 1:
                send_group(sends[0])
            runs = pieces(pair)
            total = sum(count for _, count in runs)
            for start in range(0, XB, 8):
                group = range(start, start + 8)
                if part == 0:
                    current = [stage[pl.ds(x, 128, stride=XB), :] for x in group]
                    for x, c in zip(group, current):
                        operands[x] = jnp.concatenate(
                            [c] + [pltpu.roll(c, 32 * k, 1) for k in range(1, 4)], axis=0
                        ).astype(BF16)
                product = []
                for x in group:
                    left = jnp.concatenate(
                        [
                            kick[x, pl.ds(pl.multiple_of(128 * j + first, 16), count), :]
                            for j in range(4)
                            for first, count in runs
                        ],
                        axis=0,
                    )
                    product.append(dot(left, operands[x]))
                for x, q in zip(group, product):
                    change = q[0:total]
                    for j in range(1, 4):
                        change = jnp.where(lane_block[0:total] == j, q[total * j : total * j + total], change)
                    done = 0
                    for first, count in runs:
                        at = pl.ds(XB * first + x, count, stride=XB)
                        kicked[at, :] = stage[at, :] + change[done : done + count]
                        done += count
            for first, count in runs:
                block = kicked[pl.ds(pl.multiple_of(XB * first, 256), XB * count), :]
                to_lines[pl.ds(first, count)] = block.astype(BF16).reshape(count, XB, 128)
        send_group(sends[1])
        keep()

    build_kicks(4, 10)
    wait_lines(0)
    advect(0, half, 64)
    build_kicks(10, 16)
    wait_rows(0)
    kick_rows(
        0,
        lambda pair: [(64 * pair, 64)],
        (far, near),
        lambda group: send_to_lines(1, group),
        lambda: keep_lines(1),
    )
    wait_lines(1)
    wait_sent(1)
    advect(1, double, 128)
    wait_rows(1)
    kick_rows(
        1,
        lambda pair: [(32 * h + 16 * pair, 16) for h in range(4)],
        (far_gy, near_gy),
        send_last_lines,
        keep_last_lines,
    )
    pltpu.make_async_copy(last_lines, last_lines, recv.at[4]).wait()
    advect_last()
    wait_sent(3)
    wait_sent(4, PARTS - 4)
    pltpu.make_async_copy(last_rows, last_rows, recv.at[5]).wait()
    stage[...] = last_rows[...].reshape(PARTS * XB, 128).astype(F32)
    for x in range(XB):
        current = stage[pl.ds(x, 128, stride=XB), :].astype(BF16)
        turned = nt_dot(eye, current).astype(BF16)
        for j in range(4):
            out[x, :, 128 * j : 128 * j + 128] = turned[32 * j : 32 * j + 32, :]
    wait_sent(5, PARTS - 4)


def on_device(density, kernel, electrode, drift_sign):
    vmem = pl.BlockSpec(memory_space=pltpu.VMEM)
    smem = pl.BlockSpec(memory_space=pltpu.SMEM)
    final = pl.pallas_call(
        whole_kernel,
        out_shape=jax.ShapeDtypeStruct(density.shape, BF16),
        in_specs=[vmem, vmem, smem, smem, vmem],
        out_specs=vmem,
        scratch_shapes=[
            pltpu.VMEM((PARTS, XB, 128), BF16),
            pltpu.VMEM((2, NX, 512), BF16),
            pltpu.VMEM((NX, 512), BF16),
            pltpu.VMEM((2, PARTS, XB, 128), BF16),
            pltpu.VMEM((PARTS * XB, 128), F32),
            pltpu.VMEM((4, NX, 128), BF16),
            pltpu.VMEM((4, NX, 128), BF16),
            pltpu.VMEM((PARTS, XB, 128), BF16),
            pltpu.VMEM((NX, NX), BF16),
            pltpu.VMEM((NX, NX), BF16),
            pltpu.VMEM((NX, NX), BF16),
            pltpu.VMEM((512, 512), BF16),
            pltpu.VMEM((PARTS * XB, 128), F32),
            pltpu.VMEM((XB, NP, 128), BF16),
            pltpu.VMEM((XB, NP, NP), BF16),
            pltpu.VMEM((NV, 1, 1024), F32),
            pltpu.SemaphoreType.DMA((6,)),
            pltpu.SemaphoreType.DMA((6,)),
        ],
        compiler_params=pltpu.CompilerParams(
            collective_id=0, has_side_effects=True, vmem_limit_bytes=56 << 20
        ),
    )(density, kernel, electrode, drift_sign, jnp.asarray(shift_kernels()))
    return final.astype(F32)


def solution(mesh):
    return jax.shard_map(
        on_device,
        mesh=mesh,
        in_specs=(P("gx", "gy", None), P(), P("gx"), P()),
        out_specs=P("gx", "gy", None),
        check_vma=False,
    )
```

```python
import functools

import jax
import jax.numpy as jnp
import numpy as np
from jax import lax
from jax.experimental import pallas as pl
from jax.experimental.pallas import tpu as pltpu
from jax.sharding import PartitionSpec as P

NX = 512
NP = 512
XB = 16
YB = 32
NV = 16
PARTS = 128
MESH = pl.DeviceIdType.MESH
F32 = jnp.float32
BF16 = jnp.bfloat16


def shift_kernels():
    k = np.arange(NX)
    kappa = np.where(k > NX // 2, k - NX, k).astype(np.int64)
    n = np.arange(NX)
    rows = np.zeros((8, NX), np.float64)
    for parity in range(2):
        p = parity
        m = (kappa * (NX // 4) * (NP - 1 - 2 * p)) % (NX * NP)
        phase = 2 * np.pi * m / (NX * NP)
        g = np.cos(2 * np.pi * ((n[:, None] * k[None, :]) % NX) / NX - phase[None, :]).sum(1) / NX
        spectrum = np.fft.fft(g)
        g2 = np.fft.ifft(spectrum * spectrum).real
        whole = 127 - p // 2
        whole2 = 255 - p
        rows[parity] = np.roll(g, -whole)[(-n) % NX]
        rows[2 + parity] = np.roll(g2, -whole2)[(-n) % NX]
    return rows.astype(np.float32)


def send_order():
    ring = lambda t: min(t, 4 - t)
    far = lambda o: ring(o // 16) + ring(o // 4 % 4) + ring(o % 4)
    return sorted(range(1, 64), key=lambda o: (-far(o), (o * 11) % 64))


ORDER = send_order()


def peers(me):
    y, z, x, core = me
    across = lax.rem(y + 2, 4)
    mate = lambda t: t + 1 - 2 * lax.rem(t, 2)
    ys = [8 * t for t in (y, mate(across), across, mate(y))]
    zs = [lax.rem(z + i, 4) for i in range(4)]
    xs = [lax.rem(x + i, 4) for i in range(4)]
    high = [t // 2 * 4 for t in xs]
    low = [lax.rem(t, 2) * 2 for t in xs]
    everyone, column = [], []
    parts = ([], []), ([], [])
    for o in ORDER:
        gx = ys[o // 16] + zs[o // 4 % 4] + high[o % 4]
        gy = low[o % 4]
        part, part_column = parts[0 if o // 16 in (1, 2) else 1]
        pair = [(gx, gy), (gx, gy + 1)]
        everyone += pair
        part += pair
        if o % 2 == 0:
            column.append(gx)
            part_column.append(gx)
    sibling = (ys[0] + zs[0] + high[0], low[0] + 1 - core)
    everyone.append(sibling)
    parts[1][0].append(sibling)
    return everyone, column, parts


def iota(shape, axis):
    return lax.broadcasted_iota(jnp.int32, shape, axis)


def nt_dot(a, b):
    return lax.dot_general(a, b, (((1,), (1,)), ((), ())), preferred_element_type=F32)


def dot(a, b):
    return jnp.dot(a, b, preferred_element_type=F32)


def whole_kernel(
    density,
    kernel,
    electrode,
    drift_sign,
    taps,
    out,
    to_lines,
    lines,
    to_rows,
    rows,
    stage,
    last_lines,
    last_out,
    last_rows,
    half,
    double,
    last,
    drift,
    kicked,
    operands,
    kick,
    offsets,
    send,
    recv,
):
    gx = lax.axis_index("gx")
    gy = lax.axis_index("gy")
    d = gx * 4 + gy
    me = (gx // 8, lax.rem(gx, 4), lax.rem(gx // 4, 2) * 2 + gy // 2, lax.rem(gy, 2))

    everyone, same_gy, ((far, far_gy), (near, near_gy)) = peers(me)
    near_pair = me[0] // 2
    far_pair = 1 - near_pair

    barrier = pltpu.get_barrier_semaphore()
    for peer in everyone:
        pl.semaphore_signal(barrier, inc=1, device_id=peer, device_id_type=MESH)

    def row_tile(ref, a, b):
        return ref.at[pl.ds(pl.multiple_of(a * XB, XB), XB), pl.ds(pl.multiple_of(b * 128, 128), 128)]

    def send_to_lines(r, group):
        for a, b in group:
            pltpu.make_async_remote_copy(
                src_ref=to_lines.at[a * 4 + b],
                dst_ref=row_tile(lines.at[r], gx, gy),
                send_sem=send.at[2 * r],
                recv_sem=recv.at[2 * r],
                device_id=(a, b),
                device_id_type=MESH,
            ).start()

    def keep_lines(r):
        pltpu.make_async_copy(to_lines.at[d], row_tile(lines.at[r], gx, gy), recv.at[2 * r]).start()

    def send_to_rows(r, group):
        for a, b in group:
            pltpu.make_async_remote_copy(
                src_ref=row_tile(to_rows, a, b),
                dst_ref=rows.at[r, d],
                send_sem=send.at[2 * r + 1],
                recv_sem=recv.at[2 * r + 1],
                device_id=(a, b),
                device_id_type=MESH,
            ).start()

    def keep_rows(r):
        pltpu.make_async_copy(row_tile(to_rows, gx, gy), rows.at[r, d], recv.at[2 * r + 1]).start()

    def slab(ref, a):
        return ref.at[:, pl.ds(pl.multiple_of(a * XB, XB), XB), :]

    def fan(ref, a):
        return ref.at[:, a]

    def send_last_lines(group):
        source = to_lines.reshape(4, 32, XB, 128)
        for a in group:
            pltpu.make_async_remote_copy(
                src_ref=fan(source, a),
                dst_ref=slab(last_lines, gx),
                send_sem=send.at[4],
                recv_sem=recv.at[4],
                device_id=(a, gy),
                device_id_type=MESH,
            ).start()

    def keep_last_lines():
        source = to_lines.reshape(4, 32, XB, 128)
        pltpu.make_async_copy(fan(source, gx), slab(last_lines, gx), recv.at[4]).start()

    def send_last_rows(group):
        target = last_rows.reshape(4, 32, XB, 128)
        for a in group:
            pltpu.make_async_remote_copy(
                src_ref=slab(last_out, a),
                dst_ref=fan(target, gx),
                send_sem=send.at[5],
                recv_sem=recv.at[5],
                device_id=(a, gy),
                device_id_type=MESH,
            ).start()

    def keep_last_rows():
        target = last_rows.reshape(4, 32, XB, 128)
        pltpu.make_async_copy(slab(last_out, gx), fan(target, gx), recv.at[5]).start()

    def wait_lines(r):
        pltpu.make_async_copy(lines.at[r], lines.at[r], recv.at[2 * r]).wait()

    def wait_rows(r):
        pltpu.make_async_copy(rows.at[r], rows.at[r], recv.at[2 * r + 1]).wait()

    def wait_sent(s, tiles=PARTS - 1):
        sent = to_lines.at[pl.ds(0, tiles)]
        pltpu.make_async_copy(sent, sent, send.at[s]).wait()

    eye = (iota((128, 128), 0) == iota((128, 128), 1)).astype(BF16)

    for x in range(XB):
        block = jnp.concatenate([density[x, :, 128 * j : 128 * j + 128] for j in range(4)], axis=0)
        stage[pl.ds(x, 128, stride=XB), :] = nt_dot(eye, block.astype(BF16))
    to_lines[...] = stage[0 : PARTS * XB, :].astype(BF16).reshape(PARTS, XB, 128)

    flip = (iota((512, 512), 0) == lax.rem(512 - iota((512, 512), 1), 512)).astype(BF16)
    forward = kernel[...].astype(F32)
    backward = dot(kernel[...], flip)
    ahead = jnp.where(iota((NV, 512), 1) == 0, forward, -forward)
    both = jnp.concatenate([ahead, backward], axis=1)
    for v in range(NV):
        offsets[v] = both[v : v + 1, :]

    def build_kicks(start, stop):
        for x in range(start, stop):
            base = jnp.broadcast_to(offsets[electrode[x]], (128, 1024))
            base = pltpu.roll(base, 0, 1, stride=1, stride_axis=0).astype(BF16)
            shifted = [base[:, 128 * c : 128 * c + 128] for c in range(8)]
            matrix = jnp.concatenate(
                [jnp.concatenate([shifted[(c - t) % 8] for c in range(4)], axis=1) for t in range(4)],
                axis=0,
            )
            square = dot(matrix, matrix)
            for t in range(4):
                for c in range(4):
                    at = 128 * ((t - c) % 4)
                    kick[x, 128 * t : 128 * t + 128, at : at + 128] = (
                        shifted[(c - t) % 8].astype(F32)
                        + 0.5 * square[128 * t : 128 * t + 128, 128 * c : 128 * c + 128]
                    ).astype(BF16)

    build_kicks(0, 4)
    pl.semaphore_wait(barrier, PARTS - 1)
    send_to_lines(0, everyone)
    keep_lines(0)

    parity = lax.rem(d, 2)

    def circulant(odd, row_even, row_odd, shift):
        row = jnp.where(odd == 0, row_even, row_odd)
        row = pltpu.roll(jnp.broadcast_to(row, (8, NX)), shift, 1)[0:1, :]
        wide = jnp.broadcast_to(row, (NX, NX))
        return pltpu.roll(wide, 0, 1, stride=1, stride_axis=0)

    half[...] = circulant(parity, taps[0:1, :], taps[1:2, :], NX - 127 + d // 2).astype(BF16)
    double[...] = circulant(parity, taps[2:3, :], taps[3:4, :], NX - 255 + d).astype(BF16)

    last[...] = circulant(lax.rem(gx, 2), taps[0:1, :], taps[1:2, :], NX - 127 + gx // 2).astype(BF16)

    col = iota((16, 512), 1)
    col_y = (col // 128) * 32 + lax.rem(col, 32)
    col_p = lax.rem(col // 32, 4) * 128 + d
    speed = 0.5 * ((2 * col_p - (NP - 1)).astype(F32) / NP)

    def sign_at(cell):
        slab = cell // 16
        chosen = jnp.zeros((16, 512), jnp.int32)
        for s in range(8):
            chosen = jnp.where(slab == s, drift_sign[s], chosen)
        return (2 * chosen - 1).astype(F32)

    face_low = speed * sign_at(jnp.maximum(col_y - 1, 0))
    face_high = speed * sign_at(col_y)
    keep = 1.0 - jnp.maximum(face_high, 0.0) + jnp.minimum(face_low, 0.0)
    from_next = jnp.where(col_y == 127, 0.0, -jnp.minimum(face_high, 0.0))
    from_prev = jnp.where(col_y == 0, 0.0, jnp.maximum(face_low, 0.0))
    inner = lax.rem(col, 32)
    band = jnp.where(iota((16, 512), 0) == 8, 1.0, 0.0).astype(F32)
    for _ in range(4):
        after = jnp.where(inner == 31, pltpu.roll(band, 512 - 97, 1), pltpu.roll(band, 511, 1))
        before = jnp.where(inner == 0, pltpu.roll(band, 97, 1), pltpu.roll(band, 1, 1))
        band = (
            keep * band
            + from_next * pltpu.roll(after, 1, 0)
            + from_prev * pltpu.roll(before, 15, 0)
        )
    for b in range(4):
        row = iota((128, 512), 0)
        column = iota((128, 512), 1)
        gap = (b * 32 + lax.rem(row, 32)) - ((column // 128) * 32 + lax.rem(column, 32))
        gap = jnp.where(row // 32 == lax.rem(column // 32, 4), gap, 99)
        matrix = jnp.zeros((128, 512), F32)
        for step in range(-4, 5):
            matrix = jnp.where(gap == step, band[8 + step : 9 + step, :], matrix)
        drift[128 * b : 128 * b + 128, :] = matrix.astype(BF16)

    lane_block = iota((128, 128), 1) // 32
    wide_block = lax.rem(iota((512, 512), 1) // 32, 4)

    def turn(current, block, cells):
        turned = current
        for j in range(4):
            cut = cells(j)
            moved = jnp.concatenate([current[cut:], current[:cut]], axis=0) if cut else current
            turned = jnp.where(block == j, moved, turned)
        return turned

    def advect(r, matrix, cells):
        current = dot(lines[r], drift[...]).astype(BF16)
        turned = turn(current, wide_block, lambda j: cells * j)
        for pair, group in ((far_pair, far), (near_pair, near)):
            at = pl.ds(pl.multiple_of(256 * pair, 256), 256)
            to_rows[at, :] = dot(matrix[at, :], turned).astype(BF16)
            send_to_rows(r, group)
        keep_rows(r)

    def advect_last():
        narrow = wide_block[:, :128]
        turned = [turn(last_lines[h], narrow, lambda j: 64 * j + 16 * h) for h in range(4)]
        turned = jnp.concatenate(turned, axis=1)
        for pair, group in ((far_pair, far_gy), (near_pair, near_gy)):
            at = pl.ds(pl.multiple_of(256 * pair, 256), 256)
            result = dot(last[at, :], turned).astype(BF16)
            for h in range(4):
                last_out[h, at, :] = result[:, 128 * h : 128 * h + 128]
            send_last_rows(group)
        keep_last_rows()

    def kick_rows(r, pieces, sends, send_group, keep):
        stage[0 : PARTS * XB, :] = rows[r].reshape(PARTS * XB, 128).astype(F32)
        wait_sent(2 * r)
        for part, pair in enumerate((far_pair, near_pair)):
            if part == 1:
                send_group(sends[0])
            runs = pieces(pair)
            total = sum(count for _, count in runs)
            for start in range(0, XB, 8):
                group = range(start, start + 8)
                if part == 0:
                    current = [stage[pl.ds(x, 128, stride=XB), :] for x in group]
                    for x, c in zip(group, current):
                        operands[x] = jnp.concatenate(
                            [c] + [pltpu.roll(c, 32 * k, 1) for k in range(1, 4)], axis=0
                        ).astype(BF16)
                product = []
                for x in group:
                    left = jnp.concatenate(
                        [
                            kick[x, pl.ds(pl.multiple_of(128 * j + first, 16), count), :]
                            for j in range(4)
                            for first, count in runs
                        ],
                        axis=0,
                    )
                    product.append(dot(left, operands[x]))
                for x, q in zip(group, product):
                    change = q[0:total]
                    for j in range(1, 4):
                        change = jnp.where(lane_block[0:total] == j, q[total * j : total * j + total], change)
                    done = 0
                    for first, count in runs:
                        at = pl.ds(XB * first + x, count, stride=XB)
                        kicked[at, :] = stage[at, :] + change[done : done + count]
                        done += count
            for first, count in runs:
                block = kicked[pl.ds(pl.multiple_of(XB * first, 256), XB * count), :]
                to_lines[pl.ds(first, count)] = block.astype(BF16).reshape(count, XB, 128)
        send_group(sends[1])
        keep()

    build_kicks(4, 10)
    wait_lines(0)
    advect(0, half, 64)
    build_kicks(10, 16)
    wait_rows(0)
    kick_rows(
        0,
        lambda pair: [(64 * pair, 64)],
        (far, near),
        lambda group: send_to_lines(1, group),
        lambda: keep_lines(1),
    )
    wait_lines(1)
    wait_sent(1)
    advect(1, double, 128)
    wait_rows(1)
    kick_rows(
        1,
        lambda pair: [(32 * h + 16 * pair, 16) for h in range(4)],
        (far_gy, near_gy),
        send_last_lines,
        keep_last_lines,
    )
    pltpu.make_async_copy(last_lines, last_lines, recv.at[4]).wait()
    advect_last()
    wait_sent(3)
    wait_sent(4, PARTS - 4)
    pltpu.make_async_copy(last_rows, last_rows, recv.at[5]).wait()
    stage[0 : PARTS * XB, :] = last_rows[...].reshape(PARTS * XB, 128).astype(F32)
    for x in range(XB):
        current = stage[pl.ds(x, 128, stride=XB), :].astype(BF16)
        turned = nt_dot(eye, current).astype(BF16)
        for j in range(4):
            out[x, :, 128 * j : 128 * j + 128] = turned[32 * j : 32 * j + 32, :]
    wait_sent(5, PARTS - 4)


def on_device(density, kernel, electrode, drift_sign):
    vmem = pl.BlockSpec(memory_space=pltpu.VMEM)
    smem = pl.BlockSpec(memory_space=pltpu.SMEM)
    final = pl.pallas_call(
        whole_kernel,
        out_shape=jax.ShapeDtypeStruct(density.shape, BF16),
        in_specs=[vmem, vmem, smem, smem, vmem],
        out_specs=vmem,
        scratch_shapes=[
            pltpu.VMEM((PARTS, XB, 128), BF16),
            pltpu.VMEM((2, NX, 512), BF16),
            pltpu.VMEM((NX, 512), BF16),
            pltpu.VMEM((2, PARTS, XB, 128), BF16),
            pltpu.VMEM((PARTS * XB + XB, 128), F32),
            pltpu.VMEM((4, NX, 128), BF16),
            pltpu.VMEM((4, NX, 128), BF16),
            pltpu.VMEM((PARTS, XB, 128), BF16),
            pltpu.VMEM((NX, NX), BF16),
            pltpu.VMEM((NX, NX), BF16),
            pltpu.VMEM((NX, NX), BF16),
            pltpu.VMEM((512, 512), BF16),
            pltpu.VMEM((PARTS * XB + XB, 128), F32),
            pltpu.VMEM((XB, NP, 128), BF16),
            pltpu.VMEM((XB, NP, NP), BF16),
            pltpu.VMEM((NV, 1, 1024), F32),
            pltpu.SemaphoreType.DMA((6,)),
            pltpu.SemaphoreType.DMA((6,)),
        ],
        compiler_params=pltpu.CompilerParams(
            collective_id=0, has_side_effects=True, vmem_limit_bytes=56 << 20
        ),
    )(density, kernel, electrode, drift_sign, jnp.asarray(shift_kernels()))
    return final.astype(F32)


def solution(mesh):
    return jax.shard_map(
        on_device,
        mesh=mesh,
        in_specs=(P("gx", "gy", None), P(), P("gx"), P()),
        out_specs=P("gx", "gy", None),
        check_vma=False,
    )
```
